128 devices in a mesh: clip: 8 (over x, z_lo), head: 16 (over z_hi, y, core).
Axes of the slice: x: 4, y: 4, z: 4 (z_hi: 2, z_lo: 2; z = z_hi * 2 + z_lo), core: 2. Of those that a mesh axis runs over, the one named last changes fastest.
Arguments:
- queries: bfloat16 [16384, 4096], P(('clip', 'head')), may hold values from -6 to 6
- key_rows: bfloat16 [16384, 4096], P(('clip', 'head')), may hold values from -6 to 6
- value_rows: bfloat16 [16384, 4096], P(('clip', 'head')), may hold values from -6 to 6
- query_tangent: bfloat16 [16384, 4096], P(('clip', 'head')), may hold values from -6 to 6
- key_tangent: bfloat16 [16384, 4096], P(('clip', 'head')), may hold values from -6 to 6
- value_tangent: bfloat16 [16384, 4096], P(('clip', 'head')), may hold values from -6 to 6
- partners: int32 [16, 2], replicated, may hold values from 0 to 15, as said below
- cotangent: bfloat16 [16384, 3072], P('clip'), may hold values from -6 to 6
Outputs:
- attended: bfloat16 [16384, 4096], P(('clip', 'head'))
- attended_tangent: bfloat16 [16384, 4096], P(('clip', 'head'))
- weight_grad: float32 [3072, 4096], P('clip', 'head')
The draws below stay inside these ranges and needn't reach their ends.
Inputs may be any that keep to these rules, and one draw needn't show every extreme that they name: `partners`: for clip c the two entries are distinct clips (c - d) mod 16 with 1 <= d <= 2 + c % 2.
All inputs are finite; a program needn't handle non-finite values.
Results may differ from the reference program's by a relative error of at most 0.0051.
Values may be sent and summed in bfloat16 or wider, within the bound.
No kernel may reach another device: no remote copies, remote signals or barrier semaphores. Data moves between devices by JAX's collectives and lax.ppermute only.
A program may use at most 192 MiB of HBM per device.

```python
import jax
import jax.numpy as jnp
from jax import lax

HEADS = 32
HDIM = 128
DOUT = 3072
CLIP = 1024
CLIPS_DEV = 2
CLIPS = 16
TOKENS = 16384
QW = 4096


def shared_rows(key):
    base_q = jnp.clip(jax.random.normal(jax.random.fold_in(key, 11), (TOKENS, QW), jnp.float32), -6.0, 6.0)
    base_k = jnp.clip(jax.random.normal(jax.random.fold_in(key, 12), (TOKENS, QW), jnp.float32), -6.0, 6.0)
    return (base_q, base_k)


def draw_queries(key, part):
    return shared_rows(key)[0].astype(jnp.bfloat16)


def draw_key_rows(key, part):
    return shared_rows(key)[1].astype(jnp.bfloat16)


def draw_partners(key, part):
    clip_ids = jnp.arange(CLIPS, dtype=jnp.int32)
    gap_reach = CLIPS_DEV + clip_ids % CLIPS_DEV
    first_gap = jax.random.randint(jax.random.fold_in(key, 21), (CLIPS,), 0, 1 << 20) % gap_reach + 1
    gap_step = jax.random.randint(jax.random.fold_in(key, 22), (CLIPS,), 0, 1 << 20) % (gap_reach - 1) + 1
    second_gap = (first_gap - 1 + gap_step) % gap_reach + 1
    return jnp.stack([(clip_ids - first_gap) % CLIPS, (clip_ids - second_gap) % CLIPS], axis=1).astype(jnp.int32)


def spiked(result, key, source, target, shards_of, factor):
    def block_of(axis_at):
        return (jnp.arange(result.shape[axis_at]) // (result.shape[axis_at] // shards_of)).reshape((-1,) + (1,) * (result.ndim - 1 - axis_at))

    near = jax.random.permutation(key, shards_of)[block_of(target)]
    other_side = (block_of(target) + shards_of // 2) % shards_of
    return jnp.where((block_of(source) == near) | (block_of(source) == other_side), factor * result, result)


def steps_of(key, shape, shards, smallest, top_value):
    loudness = 1.0
    for dim, parts in shards:
        draws = jax.random.uniform(jax.random.fold_in(jax.random.fold_in(key, 6), dim), (parts,), jnp.float32, smallest / len(shards), top_value / len(shards))
        loudness = loudness * jnp.repeat(jnp.exp(draws), shape[dim] // parts).reshape((-1,) + (1,) * (len(shape) - 1 - dim))
    return loudness


def gaussian(stream_key, dims, width, limit, split=(), kind=jnp.bfloat16):
    entries = width * jax.random.normal(stream_key, dims, jnp.float32)
    if split:
        entries = entries * steps_of(stream_key, dims, split, -0.22, 0.18)
    return jnp.clip(entries, -limit, limit).astype(kind)


def bell_draw_with(own_key, extent, width, reach, cuts, heavy, kind=jnp.bfloat16):
    result = width * jax.random.normal(own_key, extent, jnp.float32)
    if cuts:
        result = result * steps_of(own_key, extent, cuts, -0.22, 0.18)
    return jnp.clip(spiked(result, jax.random.fold_in(own_key, 3), *heavy), -reach, reach).astype(kind)


def setup_inputs(seed: int = 0) -> dict:
    arg_keys = jax.random.split(jax.random.key(seed), 9)
    queries = draw_queries(jax.random.fold_in(arg_keys[8], 71), 0)
    key_rows = draw_key_rows(jax.random.fold_in(arg_keys[8], 71), 0)
    value_rows = gaussian(arg_keys[2], (TOKENS, QW), 1.0, 6.0, ((0, 128),))
    query_tangent = gaussian(arg_keys[3], (TOKENS, QW), 1.0, 6.0, ((0, 128),))
    key_tangent = gaussian(arg_keys[4], (TOKENS, QW), 1.0, 6.0, ((0, 128),))
    value_tangent = gaussian(arg_keys[5], (TOKENS, QW), 1.0, 6.0, ((0, 128),))
    partners = draw_partners(jax.random.fold_in(arg_keys[8], 71), 0)
    cotangent = bell_draw_with(arg_keys[7], (TOKENS, DOUT), 1.0, 6.0, ((0, 8),), (0, 1, 8, 2.0))
    return dict(queries=queries, key_rows=key_rows, value_rows=value_rows, query_tangent=query_tangent, key_tangent=key_tangent, value_tangent=value_tangent, partners=partners, cotangent=cotangent)


def attend_head(query_part, qtan_part, key_win, value_win, ktan_win, vtan_win):
    score_scale = HDIM ** -0.5
    scores = jnp.dot(query_part, key_win.T, preferred_element_type=jnp.float32) * score_scale
    score_tan = (jnp.dot(qtan_part, key_win.T, preferred_element_type=jnp.float32)
                 + jnp.dot(query_part, ktan_win.T, preferred_element_type=jnp.float32)) * score_scale
    row_max = jnp.max(scores, axis=-1, keepdims=True)
    raw_weights = jnp.exp(scores - row_max)
    row_total = jnp.sum(raw_weights, axis=-1, keepdims=True)
    probability = raw_weights / row_total
    tangent_mean = jnp.sum(probability * score_tan, axis=-1, keepdims=True)
    prob_tangent = probability * (score_tan - tangent_mean)
    prob_low = probability.astype(jnp.bfloat16)
    tangent_low = prob_tangent.astype(jnp.bfloat16)
    result_out = jnp.dot(prob_low, value_win, preferred_element_type=jnp.float32)
    tangent_out = (jnp.dot(tangent_low, value_win, preferred_element_type=jnp.float32)
                   + jnp.dot(prob_low, vtan_win, preferred_element_type=jnp.float32))
    return result_out.astype(jnp.bfloat16), tangent_out.astype(jnp.bfloat16)


def reference(queries, key_rows, value_rows, query_tangent, key_tangent, value_tangent, partners, cotangent):
    def split_heads(array):
        return array.reshape(CLIPS, CLIP, HEADS, HDIM)

    queries4 = split_heads(queries)
    keys4 = split_heads(key_rows)
    values4 = split_heads(value_rows)
    qtan4 = split_heads(query_tangent)
    ktan4 = split_heads(key_tangent)
    vtan4 = split_heads(value_tangent)

    def one_clip(clip_index):
        partner_row = partners[clip_index]
        chosen = jnp.stack([clip_index, partner_row[0], partner_row[1]]).astype(jnp.int32)

        def window(array):
            return jnp.take(array, chosen, axis=0).reshape(3 * CLIP, HEADS, HDIM)

        key_win = window(keys4)
        value_win = window(values4)
        ktan_win = window(ktan4)
        vtan_win = window(vtan4)
        query_clip = queries4[clip_index]
        qtan_clip = qtan4[clip_index]

        def one_head(head_index):
            return attend_head(jnp.take(query_clip, head_index, axis=1), jnp.take(qtan_clip, head_index, axis=1),
                               jnp.take(key_win, head_index, axis=1), jnp.take(value_win, head_index, axis=1),
                               jnp.take(ktan_win, head_index, axis=1), jnp.take(vtan_win, head_index, axis=1))

        head_out, head_tan = lax.map(one_head, jnp.arange(HEADS, dtype=jnp.int32))
        return jnp.transpose(head_out, (1, 0, 2)), jnp.transpose(head_tan, (1, 0, 2))

    clip_out, clip_tan = lax.map(one_clip, jnp.arange(CLIPS, dtype=jnp.int32))
    attended = clip_out.reshape(TOKENS, QW)
    attended_tangent = clip_tan.reshape(TOKENS, QW)
    weight_grad = lax.dot_general(cotangent, attended, (((0,), (0,)), ((), ())), preferred_element_type=jnp.float32)
    return attended, attended_tangent, weight_grad
```

```python
import functools

import jax
import jax.numpy as jnp
import numpy as np
from jax import lax
from jax.experimental import pallas as pl
from jax.experimental.pallas import tpu as pltpu
from jax.sharding import Mesh
from jax.sharding import PartitionSpec as P

HDIM = 128
CLIP = 1024
BLOCK = 256
LOG2E = 1.4426950408889634
PLANE = ("zl", "zh", "y", "c")
GROUP = ("zh", "y", "c")
CLIPS = ("x", "zl")
EVERY = ("x", "zl", "zh", "y", "c")


def attend_kernel(slots_ref, q_ref, own_ref, *rest, loads):
    halo_ref = rest[0] if len(rest) == 7 else None
    out_ref, tan_ref, kv, scores, tangents, sem = rest[-6:]
    scale = HDIM**-0.5
    clip, block = pl.program_id(0), pl.program_id(1)

    @pl.when((clip == 0) & (block == 0))
    def _():
        copies = [
            pltpu.make_async_copy(
                (halo_ref if from_halo else own_ref).at[pl.ds(source, count)],
                kv.at[pl.ds(target, count)],
                sem.at[n],
            )
            for n, (from_halo, source, target, count) in enumerate(loads)
        ]
        for copy in copies:
            copy.start()
        for copy in copies:
            copy.wait()

    both = q_ref[0]
    query = both[:, HDIM:]
    top = jnp.full((BLOCK, HDIM), -jnp.inf, jnp.float32)
    picks = [slots_ref[clip, n] for n in range(3)]
    nt = (((1,), (1,)), ((), ()))
    for n, pick in enumerate(picks):
        part = lax.dot_general(query, kv[pick, :, :HDIM], nt, preferred_element_type=jnp.float32)
        scores[:, n * CLIP : (n + 1) * CLIP] = part
        for lane in range(0, CLIP, HDIM):
            top = jnp.maximum(top, part[:, lane : lane + HDIM])
        tangents[:, n * CLIP : (n + 1) * CLIP] = lax.dot_general(
            both, kv[pick, :, : 2 * HDIM], nt, preferred_element_type=jnp.float32
        )
    top = jnp.max(top, axis=1, keepdims=True)
    total = jnp.zeros((BLOCK, HDIM), jnp.float32)
    mean = jnp.zeros((BLOCK, HDIM), jnp.float32)
    for lane in range(0, 3 * CLIP, HDIM):
        part = jnp.exp2((scores[:, lane : lane + HDIM] - top) * (scale * LOG2E))
        total += part
        mean += part * tangents[:, lane : lane + HDIM]
        scores[:, lane : lane + HDIM] = part
    inverse = 1.0 / jnp.sum(total, axis=1, keepdims=True)
    mean = jnp.sum(mean, axis=1, keepdims=True) * inverse
    out = jnp.zeros((BLOCK, 2 * HDIM), jnp.float32)
    tan = jnp.zeros((BLOCK, HDIM), jnp.float32)
    for n, pick in enumerate(picks):
        weight = scores[:, n * CLIP : (n + 1) * CLIP]
        weight_tan = weight * (tangents[:, n * CLIP : (n + 1) * CLIP] - mean)
        out += jnp.dot(
            weight.astype(jnp.bfloat16),
            kv[pick, :, 2 * HDIM :],
            preferred_element_type=jnp.float32,
        )
        tan += jnp.dot(
            weight_tan.astype(jnp.bfloat16),
            kv[pick, :, 2 * HDIM : 3 * HDIM],
            preferred_element_type=jnp.float32,
        )
    out_ref[0] = (out[:, :HDIM] * inverse).astype(jnp.bfloat16)
    tan_ref[0] = ((tan * scale + out[:, HDIM:]) * inverse).astype(jnp.bfloat16)


def attend(slots, queries, own, halo, first, loads):
    kept = [q for q in (own, halo) if q is not None]
    spec = pl.BlockSpec((1, BLOCK, HDIM), lambda i, j, s: (i, j, 0))
    shape = jax.ShapeDtypeStruct((2, CLIP, HDIM), jnp.bfloat16)
    return pl.pallas_call(
        functools.partial(attend_kernel, loads=loads),
        out_shape=(shape, shape),
        grid_spec=pltpu.PrefetchScalarGridSpec(
            num_scalar_prefetch=1,
            grid=(2, CLIP // BLOCK),
            in_specs=[pl.BlockSpec((1, BLOCK, 2 * HDIM), lambda i, j, s: (first + i, j, 0))]
            + [pl.BlockSpec(memory_space=pl.ANY)] * len(kept),
            out_specs=(spec, spec),
            scratch_shapes=[
                pltpu.VMEM((4, CLIP, 4 * HDIM), jnp.bfloat16),
                pltpu.VMEM((BLOCK, 3 * CLIP), jnp.float32),
                pltpu.VMEM((BLOCK, 3 * CLIP), jnp.float32),
                pltpu.SemaphoreType.DMA((len(loads),)),
            ],
        ),
        compiler_params=pltpu.CompilerParams(
            dimension_semantics=("arbitrary", "arbitrary"), vmem_limit_bytes=40 << 20
        ),
        cost_estimate=pl.CostEstimate(
            flops=2 * 2 * CLIP * 3 * CLIP * HDIM * 8,
            transcendentals=2 * CLIP * 3 * CLIP,
            bytes_accessed=8 << 20,
        ),
    )(slots, queries, *kept)


def to_heads(*arrays):
    rows = arrays[0].shape[0]
    cut = [a.reshape(rows, 16, 2, HDIM) for a in arrays]
    sent = jnp.concatenate(cut, axis=3).transpose(2, 1, 0, 3)
    got = lax.all_to_all(
        sent.reshape(32, rows, -1), PLANE, split_axis=0, concat_axis=0, tiled=True
    )
    return got.reshape(4, CLIP, -1)


def on_device(
    queries, key_rows, value_rows, query_tangent, key_tangent, value_tangent, partners, cotangent
):
    own = to_heads(key_rows, key_tangent, value_rows, value_tangent)
    halo = lax.ppermute(own[2:], "x", [(i, (i + 1) % 4) for i in range(4)])
    query = to_heads(query_tangent, queries)

    plane = lax.axis_index("x") * 4
    mine = lax.dynamic_slice_in_dim(partners, plane, 4, 0)
    near = (mine - plane + 2) % 16
    slots = jnp.concatenate([jnp.arange(2, 6, dtype=jnp.int32)[:, None], near], axis=1)
    late, late_tan = attend(slots[2:] - 2, query, own, None, 2, ((False, 0, 0, 4),))
    early, early_tan = attend(
        slots[:2], query, own, halo, 0, ((True, 0, 0, 2), (False, 0, 2, 2))
    )
    pair = lax.all_to_all(
        jnp.stack([early, late]).reshape(2, 2 * CLIP, HDIM), "zl", 0, 0, tiled=True
    )
    term = lax.dot_general(
        cotangent,
        pair.transpose(1, 0, 2).reshape(2 * CLIP, 2 * HDIM),
        (((0,), (0,)), ((), ())),
        preferred_element_type=jnp.float32,
    )
    term = term.astype(jnp.bfloat16).reshape(8, -1, 2 * HDIM)
    pieces = lax.all_to_all(term, CLIPS, 0, 0, tiled=True)
    weight_grad = jnp.sum(pieces.astype(jnp.float32), axis=0)

    def to_tokens(a, axes):
        got = lax.all_to_all(a, axes, 0, 0, tiled=True)
        return got

    rows = queries.shape[0]
    att = jnp.stack(
        [early.reshape(16, rows, HDIM), late.reshape(16, rows, HDIM)]
    ).reshape(32, rows, HDIM)
    tan = jnp.stack(
        [early_tan.reshape(16, rows, HDIM), late_tan.reshape(16, rows, HDIM)]
    ).reshape(32, rows, HDIM)
    back = to_tokens(jnp.stack([att, tan], axis=1), PLANE)
    back = back.reshape(2, 16, 2, rows, HDIM).transpose(2, 3, 1, 0, 4).reshape(2, rows, 32 * HDIM)
    return back[0], back[1], weight_grad


def solution(mesh):
    shape = (4, 2, 2, 4, 2)
    fine = Mesh(np.asarray(mesh.devices).reshape(shape), EVERY)
    rows = P(EVERY, None)
    return jax.shard_map(
        on_device,
        mesh=fine,
        in_specs=(rows, rows, rows, rows, rows, rows, P(), P(CLIPS, None)),
        out_specs=(rows, rows, P(CLIPS, GROUP)),
        check_vma=False,
    )
```

```python
import functools

import jax
import jax.numpy as jnp
import numpy as np
from jax import lax
from jax.experimental import pallas as pl
from jax.experimental.pallas import tpu as pltpu
from jax.sharding import Mesh
from jax.sharding import PartitionSpec as P

HDIM = 128
CLIP = 1024
HEADS = 32
HALF = 64
SENDERS = 8
BLOCK = SENDERS * HALF
TILE = 256
LOG2E = 1.4426950408889634
PLANE = ("zl", "zh", "y", "c")
GROUP = ("zh", "y", "c")
CLIPS = ("x", "zl")
EVERY = ("x", "zl", "zh", "y", "c")
NT = (((1,), (1,)), ((), ()))
bf16, f32 = jnp.bfloat16, jnp.float32


def pack_kernel(*refs):
    *ins, out = refs
    for n, ref in enumerate(ins):
        for head in range(4):
            out[head % 2, head // 2, :, n * HDIM : (n + 1) * HDIM] = ref[
                :, head * HDIM : (head + 1) * HDIM
            ]


def to_heads(*arrays):
    rows, width = arrays[0].shape[0], len(arrays) * HDIM
    sent = pl.pallas_call(
        pack_kernel,
        out_shape=jax.ShapeDtypeStruct((2, 16, rows, width), bf16),
        grid=(8,),
        in_specs=[pl.BlockSpec((rows, 4 * HDIM), lambda j: (0, j))] * len(arrays),
        compiler_params=pltpu.CompilerParams(vmem_limit_bytes=60 << 20),
        out_specs=pl.BlockSpec((2, 2, rows, width), lambda j: (0, j, 0, 0)),
        cost_estimate=pl.CostEstimate(
            flops=0, transcendentals=0, bytes_accessed=4 * rows * HEADS * width
        ),
    )(*arrays)
    return lax.all_to_all(sent.reshape(32, rows, width), PLANE, 0, 0, tiled=True)


def unpack_kernel(first_ref, second_ref, out_ref, tan_ref):
    for half, ref in enumerate((first_ref, second_ref)):
        rows = slice(half * HALF, (half + 1) * HALF)
        for head in range(4):
            lanes = slice(head * HDIM, (head + 1) * HDIM)
            out_ref[rows, lanes] = ref[head % 2, head // 2, :, :HDIM]
            tan_ref[rows, lanes] = ref[head % 2, head // 2, :, HDIM:]


def unpack(first, second):
    shape = jax.ShapeDtypeStruct((2 * HALF, HEADS * HDIM), bf16)
    spec = pl.BlockSpec((2 * HALF, 4 * HDIM), lambda j: (0, j))
    return pl.pallas_call(
        unpack_kernel,
        out_shape=(shape, shape),
        grid=(8,),
        in_specs=[pl.BlockSpec((2, 2, HALF, 2 * HDIM), lambda j: (0, j, 0, 0))] * 2,
        out_specs=(spec, spec),
        cost_estimate=pl.CostEstimate(flops=0, transcendentals=0, bytes_accessed=4 << 20),
    )(first.reshape(2, 16, HALF, 2 * HDIM), second.reshape(2, 16, HALF, 2 * HDIM))


def attend_kernel(slots_ref, q_ref, *rest, loads, sources, halves, first_half):
    kept, rest = rest[:sources], rest[sources:]
    *outs, kv, scores, tangents, sem = rest
    outs = outs if halves == 2 else outs[-2:]
    scale = HDIM**-0.5
    half, clip = pl.program_id(0), pl.program_id(1)
    start = (half == 0) & (clip == 0)
    split = 2 * HDIM

    def copies(part):
        lanes = pl.ds(part * split, split)
        return [
            pltpu.make_async_copy(
                kept[which].at[pl.ds(source * SENDERS, count * SENDERS), :, lanes],
                kv.at[pl.ds(target * SENDERS, count * SENDERS), :, lanes],
                sem.at[part, n],
            )
            for n, (which, source, target, count) in enumerate(loads)
        ]

    @pl.when(start)
    def _():
        for copy in copies(0) + copies(1):
            copy.start()
        for copy in copies(0):
            copy.wait()

    both = q_ref[...].reshape(BLOCK, 2 * HDIM)
    query = both[:, HDIM:]
    picks = [slots_ref[clip, n] * SENDERS for n in range(3)]
    tiles = [(n, k) for n in range(3) for k in range(0, CLIP, TILE)]

    def window(n, k, lanes):
        rows = pl.ds(picks[n] + k // 128, TILE // 128)
        return kv[rows, :, lanes].reshape(TILE, -1)

    top = None
    for n, k in tiles:
        part = lax.dot_general(query, window(n, k, slice(0, HDIM)), NT, preferred_element_type=f32)
        at = n * CLIP + k
        scores[:, at : at + TILE] = part
        for lane in range(0, TILE, HDIM):
            piece = part[:, lane : lane + HDIM]
            top = piece if top is None else jnp.maximum(top, piece)
    top = jnp.broadcast_to(jnp.max(top, axis=1, keepdims=True), (BLOCK, HDIM))
    total = jnp.zeros((BLOCK, HDIM), f32)
    mean = jnp.zeros((BLOCK, HDIM), f32)
    for n, k in tiles:
        tangent = lax.dot_general(
            both, window(n, k, slice(0, 2 * HDIM)), NT, preferred_element_type=f32
        )
        for lane in range(0, TILE, HDIM):
            at = n * CLIP + k + lane
            part = jnp.exp2((scores[:, at : at + HDIM] - top) * (scale * LOG2E))
            moved = part * tangent[:, lane : lane + HDIM]
            total += part
            mean += moved
            scores[:, at : at + HDIM] = part
            tangents[:, at : at + HDIM] = moved
    inverse = 1.0 / jnp.sum(total, axis=1, keepdims=True)
    mean = jnp.broadcast_to(jnp.sum(mean, axis=1, keepdims=True) * inverse, (BLOCK, HDIM))

    @pl.when(start)
    def _():
        for copy in copies(1):
            copy.wait()

    out = jnp.zeros((BLOCK, 2 * HDIM), f32)
    tan = jnp.zeros((BLOCK, HDIM), f32)
    for n, k in tiles:
        weights, weights_tan = [], []
        for lane in range(0, TILE, HDIM):
            at = n * CLIP + k + lane
            part = scores[:, at : at + HDIM]
            weights.append(part.astype(bf16))
            weights_tan.append((tangents[:, at : at + HDIM] - part * mean).astype(bf16))
        out += jnp.dot(
            jnp.concatenate(weights, axis=1),
            window(n, k, slice(2 * HDIM, 4 * HDIM)),
            preferred_element_type=f32,
        )
        tan += jnp.dot(
            jnp.concatenate(weights_tan, axis=1),
            window(n, k, slice(2 * HDIM, 3 * HDIM)),
            preferred_element_type=f32,
        )
    result = (out[:, :HDIM] * inverse).astype(bf16).reshape(SENDERS, HALF, HDIM)
    result_tan = ((tan * scale + out[:, HDIM:]) * inverse).astype(bf16)
    result_tan = result_tan.reshape(SENDERS, HALF, HDIM)

    def store(pair_ref, sent_ref):
        pair_ref[...] = result
        sent_ref[:, :, :HDIM] = result
        sent_ref[:, :, HDIM:] = result_tan

    if halves == 1:
        store(*outs)
    else:
        pl.when(half == 0)(lambda: store(outs[0], outs[1]))
        pl.when(half == 1)(lambda: store(outs[2], outs[3]))


def attend(slots, queries, kept, loads, late, first_half, halves, filled=None):
    first = 2 if late else 0
    pair_shape = jax.ShapeDtypeStruct((16, HALF, HDIM), bf16)
    sent_shape = jax.ShapeDtypeStruct((32, HALF, 2 * HDIM), bf16)
    in_specs = [
        pl.BlockSpec((SENDERS, HALF, 2 * HDIM), lambda h, c, s: (first + c, first_half + h, 0))
    ] + [pl.BlockSpec(memory_space=pl.ANY)] * (len(kept) + (filled is not None))
    out_shape, out_specs = [], []
    for n in range(halves):

        def place(h, c, n=n):
            return c if halves == 1 else jnp.where(h == n, c, 1 - n)

        out_shape += [pair_shape, sent_shape]
        out_specs += [
            pl.BlockSpec((SENDERS, HALF, HDIM), lambda h, c, s, p=place: (p(h, c), 0, 0)),
            pl.BlockSpec(
                (SENDERS, HALF, 2 * HDIM), lambda h, c, s, p=place: (first + p(h, c), 0, 0)
            ),
        ]
    operands = (slots, queries, *kept) + (() if filled is None else (filled,))
    return pl.pallas_call(
        functools.partial(
            attend_kernel,
            loads=loads,
            sources=len(kept) + (filled is not None),
            halves=halves,
            first_half=first_half,
        ),
        out_shape=out_shape,
        grid_spec=pltpu.PrefetchScalarGridSpec(
            num_scalar_prefetch=1,
            grid=(halves, 2),
            in_specs=in_specs,
            out_specs=out_specs,
            scratch_shapes=[
                pltpu.VMEM((4 * SENDERS, 128, 4 * HDIM), bf16),
                pltpu.VMEM((BLOCK, 3 * CLIP), f32),
                pltpu.VMEM((BLOCK, 3 * CLIP), f32),
                pltpu.SemaphoreType.DMA((2, len(loads))),
            ],
        ),
        input_output_aliases={} if filled is None else {len(operands) - 1: 1},
        compiler_params=pltpu.CompilerParams(
            dimension_semantics=("arbitrary", "arbitrary"), vmem_limit_bytes=60 << 20
        ),
        cost_estimate=pl.CostEstimate(
            flops=2 * 2 * halves * BLOCK * 3 * CLIP * HDIM * 8,
            transcendentals=2 * halves * BLOCK * 3 * CLIP,
            bytes_accessed=8 << 20,
        ),
    )(*operands)


def grad_kernel(side_ref, own_a, own_b, got_a, got_b, late_a, late_b, cot_ref, out_ref, pair, turned, sem):
    @pl.when(pl.program_id(0) == 0)
    def _():
        def load(left, right):
            copies = []
            for column, halves in enumerate((left, right)):
                for half, ref in enumerate(halves):
                    copies.append(
                        pltpu.make_async_copy(
                            ref,
                            pair.at[:, pl.ds(half * HALF, HALF), pl.ds(column * HDIM, HDIM)],
                            sem.at[2 * column + half],
                        )
                    )
            for copy in copies:
                copy.start()
            for copy in copies:
                copy.wait()

        early = (own_a, own_b)
        far = (got_a, got_b)
        late = (late_a, late_b)
        pl.when(side_ref[0] == 0)(lambda: load(early, far))
        pl.when(side_ref[0] == 1)(lambda: load(far, late))
        turned[...] = pair[...].reshape(2 * CLIP, 2 * HDIM).T

    part = jnp.dot(turned[...], cot_ref[...], preferred_element_type=f32)
    out_ref[0] = part.T.astype(bf16)


def grad_term(side, early, got, late, cotangent):
    rows, columns = cotangent.shape
    width = columns // 8
    return pl.pallas_call(
        grad_kernel,
        out_shape=jax.ShapeDtypeStruct((8, width, 2 * HDIM), bf16),
        grid_spec=pltpu.PrefetchScalarGridSpec(
            num_scalar_prefetch=1,
            grid=(8,),
            in_specs=[pl.BlockSpec(memory_space=pl.ANY)] * 6
            + [pl.BlockSpec((rows, width), lambda j, s: (0, j))],
            out_specs=pl.BlockSpec((1, width, 2 * HDIM), lambda j, s: (j, 0, 0)),
            scratch_shapes=[
                pltpu.VMEM((16, 2 * HALF, 2 * HDIM), bf16),
                pltpu.VMEM((2 * HDIM, rows), bf16),
                pltpu.SemaphoreType.DMA((4,)),
            ],
        ),
        compiler_params=pltpu.CompilerParams(vmem_limit_bytes=60 << 20),
        cost_estimate=pl.CostEstimate(
            flops=2 * rows * columns * 2 * HDIM, transcendentals=0, bytes_accessed=15 << 20
        ),
    )(side, *early, *got, *late, cotangent)


def on_device(
    queries, key_rows, value_rows, query_tangent, key_tangent, value_tangent, partners, cotangent
):
    own = to_heads(key_rows, key_tangent, value_rows, value_tangent)
    halo = lax.ppermute(own[16:], "x", [(i, (i + 1) % 4) for i in range(4)])
    query = to_heads(query_tangent, queries)

    plane = lax.axis_index("x") * 4
    mine = lax.dynamic_slice_in_dim(partners, plane, 4, 0)
    near = (mine - plane + 2) % 16
    slots = jnp.concatenate([jnp.arange(2, 6, dtype=jnp.int32)[:, None], near], axis=1)
    late1, sent1, late2, sent2 = attend(
        slots[2:] - 2, query, (own,), ((0, 0, 0, 4),), True, 0, 2
    )
    window = ((1, 0, 0, 2), (0, 0, 2, 2))
    early1, sent1 = attend(slots[:2], query, (own, halo), window, False, 0, 1, sent1)
    early2, sent2 = attend(slots[:2], query, (own, halo), window, False, 1, 1, sent2)

    side = lax.axis_index("zl")

    def swap(late, early):
        return lax.ppermute(jnp.where(side == 0, late, early), "zl", [(0, 1), (1, 0)])

    got1, got2 = swap(late1, early1), swap(late2, early2)
    term = grad_term(side[None], (early1, early2), (got1, got2), (late1, late2), cotangent)
    back1 = lax.all_to_all(sent1, PLANE, 0, 0, tiled=True)
    sent2, _ = lax.optimization_barrier((sent2, got2))
    back2 = lax.all_to_all(sent2, PLANE, 0, 0, tiled=True)
    pieces = lax.all_to_all(term, CLIPS, 0, 0, tiled=True)
    weight_grad = jnp.sum(pieces.astype(f32), axis=0)
    attended, attended_tangent = unpack(back1, back2)
    return attended, attended_tangent, weight_grad


def solution(mesh):
    fine = Mesh(np.asarray(mesh.devices).reshape(4, 2, 2, 4, 2), EVERY)
    rows = P(EVERY, None)
    return jax.shard_map(
        on_device,
        mesh=fine,
        in_specs=(rows, rows, rows, rows, rows, rows, P(), P(CLIPS, None)),
        out_specs=(rows, rows, P(CLIPS, GROUP)),
        check_vma=False,
    )
```

```python
import functools

import jax
import jax.numpy as jnp
import numpy as np
from jax import lax
from jax.experimental import pallas as pl
from jax.experimental.pallas import tpu as pltpu
from jax.sharding import Mesh
from jax.sharding import PartitionSpec as P

HDIM = 128
CLIP = 1024
HEADS = 32
HALF = 64
SENDERS = 8
BLOCK = SENDERS * HALF
TILE = 256
LOG2E = 1.4426950408889634
PLANE = ("zl", "zh", "y", "c")
GROUP = ("zh", "y", "c")
CLIPS = ("x", "zl")
EVERY = ("x", "zl", "zh", "y", "c")
NT = (((1,), (1,)), ((), ()))
bf16, f32 = jnp.bfloat16, jnp.float32


def pack_kernel(*refs):
    count = len(refs) - 5
    ins, (out, rows, cut, arrived, left) = refs[:count], refs[count:]
    steps = arrived.shape[0]
    heads = HEADS // steps
    width = heads * HDIM
    reads = [
        [
            pltpu.make_async_copy(
                ref.at[:, pl.ds(step * width, width)],
                rows.at[n, :, pl.ds(step * width, width)],
                arrived.at[step, n],
            )
            for n, ref in enumerate(ins)
        ]
        for step in range(steps)
    ]
    for copies in reads:
        for copy in copies:
            copy.start()
    writes = []
    for step, copies in enumerate(reads):
        for n, copy in enumerate(copies):
            copy.wait()
            for head in range(step * heads, (step + 1) * heads):
                cut[head % 2, head // 2, :, n * HDIM : (n + 1) * HDIM] = rows[
                    n, :, head * HDIM : (head + 1) * HDIM
                ]
        part = pl.ds(step * heads // 2, heads // 2)
        writes.append(pltpu.make_async_copy(cut.at[:, part], out.at[:, part], left.at[step]))
        writes[-1].start()
    for copy in writes:
        copy.wait()


def to_heads(*arrays):
    count = len(arrays)
    rows, width = arrays[0].shape[0], count * HDIM
    steps = 4
    anywhere = pl.BlockSpec(memory_space=pl.ANY)
    sent = pl.pallas_call(
        pack_kernel,
        out_shape=jax.ShapeDtypeStruct((2, 16, rows, width), bf16),
        in_specs=[anywhere] * count,
        out_specs=anywhere,
        scratch_shapes=[
            pltpu.VMEM((count, rows, HEADS * HDIM), bf16),
            pltpu.VMEM((2, 16, rows, width), bf16),
            pltpu.SemaphoreType.DMA((steps, count)),
            pltpu.SemaphoreType.DMA((steps,)),
        ],
        compiler_params=pltpu.CompilerParams(vmem_limit_bytes=60 << 20),
        cost_estimate=pl.CostEstimate(
            flops=0, transcendentals=0, bytes_accessed=4 * rows * HEADS * width
        ),
    )(*arrays)
    return lax.all_to_all(sent.reshape(32, rows, width), PLANE, 0, 0, tiled=True)


def unpack_kernel(first_ref, second_ref, out_ref, tan_ref):
    for half, ref in enumerate((first_ref, second_ref)):
        rows = slice(half * HALF, (half + 1) * HALF)
        for head in range(4):
            lanes = slice(head * HDIM, (head + 1) * HDIM)
            out_ref[rows, lanes] = ref[head % 2, head // 2, :, :HDIM]
            tan_ref[rows, lanes] = ref[head % 2, head // 2, :, HDIM:]


def unpack(first, second):
    shape = jax.ShapeDtypeStruct((2 * HALF, HEADS * HDIM), bf16)
    spec = pl.BlockSpec((2 * HALF, 4 * HDIM), lambda j: (0, j))
    return pl.pallas_call(
        unpack_kernel,
        out_shape=(shape, shape),
        grid=(8,),
        in_specs=[pl.BlockSpec((2, 2, HALF, 2 * HDIM), lambda j: (0, j, 0, 0))] * 2,
        out_specs=(spec, spec),
        cost_estimate=pl.CostEstimate(flops=0, transcendentals=0, bytes_accessed=4 << 20),
    )(first.reshape(2, 16, HALF, 2 * HDIM), second.reshape(2, 16, HALF, 2 * HDIM))


def attend_kernel(slots_ref, q_ref, *rest, loads, sources, halves, first, first_half):
    kept, rest = rest[:sources], rest[sources:]
    *outs, queries, kv, scores, tangents, sem, query_sem = rest
    scale = HDIM**-0.5
    half, clip = pl.program_id(0), pl.program_id(1)
    start = (half == 0) & (clip == 0)
    split = 2 * HDIM
    blocks = [(h, c) for h in range(halves) for c in range(2)]

    def fetch(step, at):
        return pltpu.make_async_copy(
            q_ref.at[
                pl.ds((first + at[1]) * SENDERS, SENDERS),
                pl.ds((first_half + at[0]) * HALF, HALF),
            ],
            queries.at[step],
            query_sem.at[step],
        )

    def copies(part):
        lanes = pl.ds(part * split, split)
        return [
            pltpu.make_async_copy(
                kept[which].at[pl.ds(source * SENDERS, count * SENDERS), :, lanes],
                kv.at[pl.ds(target * SENDERS, count * SENDERS), :, lanes],
                sem.at[part, n],
            )
            for n, (which, source, target, count) in enumerate(loads)
        ]

    @pl.when(start)
    def _():
        fetches = [fetch(step, at) for step, at in enumerate(blocks)]
        for copy in copies(0) + fetches + copies(1):
            copy.start()
        for copy in copies(0) + fetches:
            copy.wait()

    both = queries[2 * half + clip].reshape(BLOCK, 2 * HDIM)
    query = both[:, HDIM:]
    picks = [slots_ref[clip, n] * SENDERS for n in range(3)]
    tiles = [(n, k) for n in range(3) for k in range(0, CLIP, TILE)]

    def window(n, k, lanes):
        rows = pl.ds(picks[n] + k // 128, TILE // 128)
        return kv[rows, :, lanes].reshape(TILE, -1)

    top = None
    for n, k in tiles:
        part = lax.dot_general(query, window(n, k, slice(0, HDIM)), NT, preferred_element_type=f32)
        at = n * CLIP + k
        scores[:, at : at + TILE] = part
        for lane in range(0, TILE, HDIM):
            piece = part[:, lane : lane + HDIM]
            top = piece if top is None else jnp.maximum(top, piece)
    top = jnp.broadcast_to(jnp.max(top, axis=1, keepdims=True), (BLOCK, HDIM))
    total = jnp.zeros((BLOCK, HDIM), f32)
    mean = jnp.zeros((BLOCK, HDIM), f32)
    for n, k in tiles:
        tangent = lax.dot_general(
            both, window(n, k, slice(0, 2 * HDIM)), NT, preferred_element_type=f32
        )
        for lane in range(0, TILE, HDIM):
            at = n * CLIP + k + lane
            part = jnp.exp2((scores[:, at : at + HDIM] - top) * (scale * LOG2E))
            moved = part * tangent[:, lane : lane + HDIM]
            total += part
            mean += moved
            scores[:, at : at + HDIM] = part
            tangents[:, at : at + HDIM] = moved
    inverse = 1.0 / jnp.sum(total, axis=1, keepdims=True)
    mean = jnp.broadcast_to(jnp.sum(mean, axis=1, keepdims=True) * inverse, (BLOCK, HDIM))

    @pl.when(start)
    def _():
        for copy in copies(1):
            copy.wait()

    out = jnp.zeros((BLOCK, 2 * HDIM), f32)
    tan = jnp.zeros((BLOCK, HDIM), f32)
    for n, k in tiles:
        weights, weights_tan = [], []
        for lane in range(0, TILE, HDIM):
            at = n * CLIP + k + lane
            part = scores[:, at : at + HDIM]
            weights.append(part.astype(bf16))
            weights_tan.append((tangents[:, at : at + HDIM] - part * mean).astype(bf16))
        out += jnp.dot(
            jnp.concatenate(weights, axis=1),
            window(n, k, slice(2 * HDIM, 4 * HDIM)),
            preferred_element_type=f32,
        )
        tan += jnp.dot(
            jnp.concatenate(weights_tan, axis=1),
            window(n, k, slice(2 * HDIM, 3 * HDIM)),
            preferred_element_type=f32,
        )
    result = (out[:, :HDIM] * inverse).astype(bf16).reshape(SENDERS, HALF, HDIM)
    result_tan = ((tan * scale + out[:, HDIM:]) * inverse).astype(bf16)
    result_tan = result_tan.reshape(SENDERS, HALF, HDIM)

    def store(pair_ref, sent_ref):
        pair_ref[...] = result
        sent_ref[:, :, :HDIM] = result
        sent_ref[:, :, HDIM:] = result_tan

    if halves == 1:
        store(*outs)
    else:
        pl.when(half == 0)(lambda: store(outs[0], outs[1]))
        pl.when(half == 1)(lambda: store(outs[2], outs[3]))


def attend(slots, queries, kept, loads, late, first_half, halves, filled=None):
    first = 2 if late else 0
    pair_shape = jax.ShapeDtypeStruct((16, HALF, HDIM), bf16)
    sent_shape = jax.ShapeDtypeStruct((32, HALF, 2 * HDIM), bf16)
    in_specs = [pl.BlockSpec(memory_space=pl.ANY)] * (1 + len(kept) + (filled is not None))
    out_shape, out_specs = [], []
    for n in range(halves):

        def place(h, c, n=n):
            return c if halves == 1 else jnp.where(h == n, c, 1 - n)

        out_shape += [pair_shape, sent_shape]
        out_specs += [
            pl.BlockSpec((SENDERS, HALF, HDIM), lambda h, c, s, p=place: (p(h, c), 0, 0)),
            pl.BlockSpec(
                (SENDERS, HALF, 2 * HDIM), lambda h, c, s, p=place: (first + p(h, c), 0, 0)
            ),
        ]
    operands = (slots, queries, *kept) + (() if filled is None else (filled,))
    return pl.pallas_call(
        functools.partial(
            attend_kernel,
            loads=loads,
            sources=len(kept) + (filled is not None),
            halves=halves,
            first=first,
            first_half=first_half,
        ),
        out_shape=out_shape,
        grid_spec=pltpu.PrefetchScalarGridSpec(
            num_scalar_prefetch=1,
            grid=(halves, 2),
            in_specs=in_specs,
            out_specs=out_specs,
            scratch_shapes=[
                pltpu.VMEM((2 * halves, SENDERS, HALF, 2 * HDIM), bf16),
                pltpu.VMEM((4 * SENDERS, 128, 4 * HDIM), bf16),
                pltpu.VMEM((BLOCK, 3 * CLIP), f32),
                pltpu.VMEM((BLOCK, 3 * CLIP), f32),
                pltpu.SemaphoreType.DMA((2, len(loads))),
                pltpu.SemaphoreType.DMA((2 * halves,)),
            ],
        ),
        input_output_aliases={} if filled is None else {len(operands) - 1: 1},
        compiler_params=pltpu.CompilerParams(
            dimension_semantics=("arbitrary", "arbitrary"), vmem_limit_bytes=60 << 20
        ),
        cost_estimate=pl.CostEstimate(
            flops=2 * 2 * halves * BLOCK * 3 * CLIP * HDIM * 8,
            transcendentals=2 * halves * BLOCK * 3 * CLIP,
            bytes_accessed=8 << 20,
        ),
    )(*operands)


def grad_kernel(side_ref, own_a, own_b, got_a, got_b, late_a, late_b, cot_ref, out_ref, pair, sem):
    @pl.when(pl.program_id(0) == 0)
    def _():
        def load(left, right):
            copies = []
            for column, halves in enumerate((left, right)):
                for half, ref in enumerate(halves):
                    copies.append(
                        pltpu.make_async_copy(
                            ref,
                            pair.at[:, pl.ds(half * HALF, HALF), pl.ds(column * HDIM, HDIM)],
                            sem.at[2 * column + half],
                        )
                    )
            for copy in copies:
                copy.start()
            for copy in copies:
                copy.wait()

        early = (own_a, own_b)
        far = (got_a, got_b)
        late = (late_a, late_b)
        pl.when(side_ref[0] == 0)(lambda: load(early, far))
        pl.when(side_ref[0] == 1)(lambda: load(far, late))

    part = lax.dot_general(
        cot_ref[...],
        pair[...].reshape(2 * CLIP, 2 * HDIM),
        (((0,), (0,)), ((), ())),
        preferred_element_type=f32,
    )
    out_ref[...] = part.astype(bf16).reshape(out_ref.shape)


def grad_term(side, early, got, late, cotangent):
    rows, columns = cotangent.shape
    width = columns // 8
    return pl.pallas_call(
        grad_kernel,
        out_shape=jax.ShapeDtypeStruct((8, width, 2 * HDIM), bf16),
        grid_spec=pltpu.PrefetchScalarGridSpec(
            num_scalar_prefetch=1,
            grid=(2,),
            in_specs=[pl.BlockSpec(memory_space=pl.ANY)] * 6
            + [pl.BlockSpec((rows, 4 * width), lambda j, s: (0, j))],
            out_specs=pl.BlockSpec((4, width, 2 * HDIM), lambda j, s: (j, 0, 0)),
            scratch_shapes=[
                pltpu.VMEM((16, 2 * HALF, 2 * HDIM), bf16),
                pltpu.SemaphoreType.DMA((4,)),
            ],
        ),
        compiler_params=pltpu.CompilerParams(vmem_limit_bytes=60 << 20),
        cost_estimate=pl.CostEstimate(
            flops=2 * rows * columns * 2 * HDIM, transcendentals=0, bytes_accessed=15 << 20
        ),
    )(side, *early, *got, *late, cotangent)


def on_device(
    queries, key_rows, value_rows, query_tangent, key_tangent, value_tangent, partners, cotangent
):
    own = to_heads(key_rows, key_tangent, value_rows, value_tangent)
    halo = lax.ppermute(own[16:], "x", [(i, (i + 1) % 4) for i in range(4)])
    query = to_heads(query_tangent, queries)

    plane = lax.axis_index("x") * 4
    mine = lax.dynamic_slice_in_dim(partners, plane, 4, 0)
    near = (mine - plane + 2) % 16
    slots = jnp.concatenate([jnp.arange(2, 6, dtype=jnp.int32)[:, None], near], axis=1)
    late1, sent1, late2, sent2 = attend(
        slots[2:] - 2, query, (own,), ((0, 0, 0, 4),), True, 0, 2
    )
    window = ((1, 0, 0, 2), (0, 0, 2, 2))
    early1, sent1 = attend(slots[:2], query, (own, halo), window, False, 0, 1, sent1)
    early2, sent2 = attend(slots[:2], query, (own, halo), window, False, 1, 1, sent2)

    side = lax.axis_index("zl")

    def swap(late, early, after=None):
        sent = jnp.where(side == 0, late, early)
        if after is not None:
            sent, _ = lax.optimization_barrier((sent, after))
        return lax.ppermute(sent, "zl", [(0, 1), (1, 0)])

    got1 = swap(late1, early1)
    got2 = swap(late2, early2, got1)
    term = grad_term(side[None], (early1, early2), (got1, got2), (late1, late2), cotangent)
    back1 = lax.all_to_all(sent1, PLANE, 0, 0, tiled=True)
    sent2, _ = lax.optimization_barrier((sent2, got2))
    back2 = lax.all_to_all(sent2, PLANE, 0, 0, tiled=True)
    pieces = lax.all_to_all(term, CLIPS, 0, 0, tiled=True)
    weight_grad = jnp.sum(pieces.astype(f32), axis=0)
    attended, attended_tangent = unpack(back1, back2)
    return attended, attended_tangent, weight_grad


def solution(mesh):
    fine = Mesh(np.asarray(mesh.devices).reshape(4, 2, 2, 4, 2), EVERY)
    rows = P(EVERY, None)
    return jax.shard_map(
        on_device,
        mesh=fine,
        in_specs=(rows, rows, rows, rows, rows, rows, P(), P(CLIPS, None)),
        out_specs=(rows, rows, P(CLIPS, GROUP)),
        check_vma=False,
    )
```

```python
import functools

import jax
import jax.numpy as jnp
import numpy as np
from jax import lax
from jax.experimental import pallas as pl
from jax.experimental.pallas import tpu as pltpu
from jax.sharding import Mesh
from jax.sharding import PartitionSpec as P

HDIM = 128
CLIP = 1024
HEADS = 32
HALF = 64
SENDERS = 8
BLOCK = SENDERS * HALF
TILE = 256
HOPS = (2, 1, 3, 0)
LOG2E = 1.4426950408889634
PLANE = ("zl", "zh", "y", "c")
GROUP = ("zh", "y", "c")
CLIPS = ("x", "zl")
EVERY = ("x", "zl", "zh", "y", "c")
NT = (((1,), (1,)), ((), ()))
bf16, f32 = jnp.bfloat16, jnp.float32


def pack_kernel(*refs):
    count = len(refs) - 5
    ins, (out, rows, cut, arrived, left) = refs[:count], refs[count:]
    steps = arrived.shape[0]
    heads = HEADS // steps
    width = heads * HDIM
    reads = [
        [
            pltpu.make_async_copy(
                ref.at[:, pl.ds(step * width, width)],
                rows.at[n, :, pl.ds(step * width, width)],
                arrived.at[step, n],
            )
            for n, ref in enumerate(ins)
        ]
        for step in range(steps)
    ]
    for copies in reads:
        for copy in copies:
            copy.start()
    writes = []
    for step, copies in enumerate(reads):
        for n, copy in enumerate(copies):
            copy.wait()
            for head in range(step * heads, (step + 1) * heads):
                cut[head % 2, head // 2, :, n * HDIM : (n + 1) * HDIM] = rows[
                    n, :, head * HDIM : (head + 1) * HDIM
                ]
        part = pl.ds(step * heads // 2, heads // 2)
        writes.append(pltpu.make_async_copy(cut.at[:, part], out.at[:, part], left.at[step]))
        writes[-1].start()
    for copy in writes:
        copy.wait()


def packed(*arrays):
    count = len(arrays)
    rows, width = arrays[0].shape[0], count * HDIM
    steps = 4
    anywhere = pl.BlockSpec(memory_space=pl.ANY)
    return pl.pallas_call(
        pack_kernel,
        out_shape=jax.ShapeDtypeStruct((2, 16, rows, width), bf16),
        in_specs=[anywhere] * count,
        out_specs=anywhere,
        scratch_shapes=[
            pltpu.VMEM((count, rows, HEADS * HDIM), bf16),
            pltpu.VMEM((2, 16, rows, width), bf16),
            pltpu.SemaphoreType.DMA((steps, count)),
            pltpu.SemaphoreType.DMA((steps,)),
        ],
        compiler_params=pltpu.CompilerParams(vmem_limit_bytes=60 << 20),
        cost_estimate=pl.CostEstimate(
            flops=0, transcendentals=0, bytes_accessed=4 * rows * HEADS * width
        ),
    )(*arrays).reshape(32, rows, width)


def to_heads(sent):
    return lax.all_to_all(sent, PLANE, 0, 0, tiled=True)


def unpack_kernel(ref, out_ref, tan_ref):
    for head in range(8):
        lanes = slice(head * HDIM, (head + 1) * HDIM)
        out_ref[:, lanes] = ref[head % 2, head // 2, :, :HDIM]
        tan_ref[:, lanes] = ref[head % 2, head // 2, :, HDIM:]


def unpack(back):
    rows = back.shape[1]
    shape = jax.ShapeDtypeStruct((rows, HEADS * HDIM), bf16)
    spec = pl.BlockSpec((rows, 8 * HDIM), lambda j: (0, j))
    return pl.pallas_call(
        unpack_kernel,
        out_shape=(shape, shape),
        grid=(4,),
        in_specs=[pl.BlockSpec((2, 4, rows, 2 * HDIM), lambda j: (0, j, 0, 0))],
        out_specs=(spec, spec),
        cost_estimate=pl.CostEstimate(flops=0, transcendentals=0, bytes_accessed=4 << 20),
    )(back.reshape(2, 16, rows, 2 * HDIM))


def attend_kernel(slots_ref, q_ref, *rest, loads, sources, halves, first, first_half):
    kept, rest = rest[:sources], rest[sources:]
    *outs, queries, kv, scores, tangents, sem, query_sem = rest
    scale = HDIM**-0.5
    half, clip = pl.program_id(0), pl.program_id(1)
    start = (half == 0) & (clip == 0)
    split = 2 * HDIM
    blocks = [(h, c) for h in range(halves) for c in range(2)]

    def fetch(step, at):
        return pltpu.make_async_copy(
            q_ref.at[
                pl.ds((first + at[1]) * SENDERS, SENDERS),
                pl.ds((first_half + at[0]) * HALF, HALF),
            ],
            queries.at[step],
            query_sem.at[step],
        )

    def copies(part):
        lanes = pl.ds(part * split, split)
        return [
            pltpu.make_async_copy(
                kept[which].at[pl.ds(source * SENDERS, count * SENDERS), :, lanes],
                kv.at[pl.ds(target * SENDERS, count * SENDERS), :, lanes],
                sem.at[part, n],
            )
            for n, (which, source, target, count) in enumerate(loads)
        ]

    @pl.when(start)
    def _():
        fetches = [fetch(step, at) for step, at in enumerate(blocks)]
        for copy in copies(0) + fetches + copies(1):
            copy.start()
        for copy in copies(0) + fetches:
            copy.wait()

    both = queries[2 * half + clip].reshape(BLOCK, 2 * HDIM)
    query = both[:, HDIM:]
    picks = [slots_ref[clip, n] * SENDERS for n in range(3)]
    tiles = [(n, k) for n in range(3) for k in range(0, CLIP, TILE)]

    def window(n, k, lanes):
        rows = pl.ds(picks[n] + k // 128, TILE // 128)
        return kv[rows, :, lanes].reshape(TILE, -1)

    top = None
    for n, k in tiles:
        part = lax.dot_general(query, window(n, k, slice(0, HDIM)), NT, preferred_element_type=f32)
        at = n * CLIP + k
        scores[:, at : at + TILE] = part
        for lane in range(0, TILE, HDIM):
            piece = part[:, lane : lane + HDIM]
            top = piece if top is None else jnp.maximum(top, piece)
    top = jnp.broadcast_to(jnp.max(top, axis=1, keepdims=True), (BLOCK, HDIM))
    total = jnp.zeros((BLOCK, HDIM), f32)
    mean = jnp.zeros((BLOCK, HDIM), f32)
    for n, k in tiles:
        tangent = lax.dot_general(
            both, window(n, k, slice(0, 2 * HDIM)), NT, preferred_element_type=f32
        )
        for lane in range(0, TILE, HDIM):
            at = n * CLIP + k + lane
            part = jnp.exp2((scores[:, at : at + HDIM] - top) * (scale * LOG2E))
            moved = part * tangent[:, lane : lane + HDIM]
            total += part
            mean += moved
            scores[:, at : at + HDIM] = part
            tangents[:, at : at + HDIM] = moved
    inverse = 1.0 / jnp.sum(total, axis=1, keepdims=True)
    mean = jnp.broadcast_to(jnp.sum(mean, axis=1, keepdims=True) * inverse, (BLOCK, HDIM))

    @pl.when(start)
    def _():
        for copy in copies(1):
            copy.wait()

    out = jnp.zeros((BLOCK, 2 * HDIM), f32)
    tan = jnp.zeros((BLOCK, HDIM), f32)
    for n, k in tiles:
        weights, weights_tan = [], []
        for lane in range(0, TILE, HDIM):
            at = n * CLIP + k + lane
            part = scores[:, at : at + HDIM]
            weights.append(part.astype(bf16))
            weights_tan.append((tangents[:, at : at + HDIM] - part * mean).astype(bf16))
        out += jnp.dot(
            jnp.concatenate(weights, axis=1),
            window(n, k, slice(2 * HDIM, 4 * HDIM)),
            preferred_element_type=f32,
        )
        tan += jnp.dot(
            jnp.concatenate(weights_tan, axis=1),
            window(n, k, slice(2 * HDIM, 3 * HDIM)),
            preferred_element_type=f32,
        )
    result = (out[:, :HDIM] * inverse).astype(bf16).reshape(SENDERS, HALF, HDIM)
    result_tan = ((tan * scale + out[:, HDIM:]) * inverse).astype(bf16)
    result_tan = result_tan.reshape(SENDERS, HALF, HDIM)

    pair_ref, sent_ref = outs
    pair_ref[0] = result
    sent_ref[:, :, :HDIM] = result
    sent_ref[:, :, HDIM:] = result_tan


def attend(slots, queries, kept, loads, late, first_half, halves, filled=None):
    first = 2 if late else 0
    in_specs = [pl.BlockSpec(memory_space=pl.ANY)] * (1 + len(kept) + (filled is not None))
    out_shape = (
        jax.ShapeDtypeStruct((halves, 16, HALF, HDIM), bf16),
        jax.ShapeDtypeStruct((32, 2 * HALF, 2 * HDIM), bf16),
    )
    out_specs = (
        pl.BlockSpec((1, SENDERS, HALF, HDIM), lambda h, c, s: (h, c, 0, 0)),
        pl.BlockSpec(
            (SENDERS, HALF, 2 * HDIM), lambda h, c, s: (first + c, first_half + h, 0)
        ),
    )
    operands = (slots, queries, *kept) + (() if filled is None else (filled,))
    return pl.pallas_call(
        functools.partial(
            attend_kernel,
            loads=loads,
            sources=len(kept) + (filled is not None),
            halves=halves,
            first=first,
            first_half=first_half,
        ),
        out_shape=out_shape,
        grid_spec=pltpu.PrefetchScalarGridSpec(
            num_scalar_prefetch=1,
            grid=(halves, 2),
            in_specs=in_specs,
            out_specs=out_specs,
            scratch_shapes=[
                pltpu.VMEM((2 * halves, SENDERS, HALF, 2 * HDIM), bf16),
                pltpu.VMEM((4 * SENDERS, 128, 4 * HDIM), bf16),
                pltpu.VMEM((BLOCK, 3 * CLIP), f32),
                pltpu.VMEM((BLOCK, 3 * CLIP), f32),
                pltpu.SemaphoreType.DMA((2, len(loads))),
                pltpu.SemaphoreType.DMA((2 * halves,)),
            ],
        ),
        input_output_aliases={} if filled is None else {len(operands) - 1: 1},
        compiler_params=pltpu.CompilerParams(
            dimension_semantics=("arbitrary", "arbitrary"), vmem_limit_bytes=60 << 20
        ),
        cost_estimate=pl.CostEstimate(
            flops=2 * 2 * halves * BLOCK * 3 * CLIP * HDIM * 8,
            transcendentals=2 * halves * BLOCK * 3 * CLIP,
            bytes_accessed=8 << 20,
        ),
    )(*operands)


def turn_kernel(ref, out_ref):
    out_ref[...] = ref[...].T


def turned(cotangent):
    rows, columns = cotangent.shape
    return pl.pallas_call(
        turn_kernel,
        out_shape=jax.ShapeDtypeStruct((columns, rows), bf16),
        grid=(8,),
        in_specs=[pl.BlockSpec((rows, columns // 8), lambda j: (0, j))],
        out_specs=pl.BlockSpec((columns // 8, rows), lambda j: (j, 0)),
        compiler_params=pltpu.CompilerParams(vmem_limit_bytes=32 << 20),
        cost_estimate=pl.CostEstimate(flops=0, transcendentals=0, bytes_accessed=24 << 20),
    )(cotangent)


def grad_kernel(place_ref, early_a, early_b, got_a, got_b, late, got_late, cot_ref, *rest):
    outs, (pair, rows, parts, cut, sem, arrived, left) = rest[:8], rest[8:]
    plane, side = place_ref[0], place_ref[1]
    height = 2 * parts.shape[2]
    reads = [
        pltpu.make_async_copy(
            cot_ref.at[pl.ds(pl.multiple_of((plane + dx) % 4 * height, height), height)],
            rows.at[step],
            arrived.at[step],
        )
        for step, dx in enumerate(HOPS)
    ]

    def load(left_halves, right_halves):
        copies = []
        for column, halves in enumerate((left_halves, right_halves)):
            for half, ref in enumerate(halves):
                copies.append(
                    pltpu.make_async_copy(
                        ref,
                        pair.at[:, pl.ds(half * HALF, HALF), pl.ds(column * HDIM, HDIM)],
                        sem.at[2 * column + half],
                    )
                )
        for copy in copies:
            copy.start()
        for copy in copies:
            copy.wait()

    for copy in reads:
        copy.start()
    halves = lambda ref: (ref.at[0], ref.at[1])
    own = (early_a.at[0], early_b.at[0])
    far = (got_a.at[0], got_b.at[0])
    pl.when(side == 0)(lambda: load(own, far))
    pl.when(side == 1)(lambda: load(halves(got_late), halves(late)))
    writes = []
    for step, copy in enumerate(reads):
        copy.wait()
        part = jnp.dot(
            rows[step], pair[...].reshape(2 * CLIP, 2 * HDIM), preferred_element_type=f32
        )
        parts[step] = part.astype(bf16).reshape(2, height // 2, 2 * HDIM)
        for dz in range(2):
            n = 2 * step + dz
            cut[n] = parts[step, side ^ dz]
            writes.append(pltpu.make_async_copy(cut.at[n], outs[n], left.at[n]))
            writes[-1].start()
    for copy in writes:
        copy.wait()


def grad_terms(place, attended, cotangent):
    columns, rows = cotangent.shape
    width = columns // 8
    anywhere = pl.BlockSpec(memory_space=pl.ANY)
    return pl.pallas_call(
        grad_kernel,
        out_shape=[jax.ShapeDtypeStruct((width, 2 * HDIM), bf16)] * 8,
        grid_spec=pltpu.PrefetchScalarGridSpec(
            num_scalar_prefetch=1,
            grid=(),
            in_specs=[anywhere] * 7,
            out_specs=[anywhere] * 8,
            scratch_shapes=[
                pltpu.VMEM((16, 2 * HALF, 2 * HDIM), bf16),
                pltpu.VMEM((4, 2 * width, rows), bf16),
                pltpu.VMEM((4, 2, width, 2 * HDIM), bf16),
                pltpu.VMEM((8, width, 2 * HDIM), bf16),
                pltpu.SemaphoreType.DMA((4,)),
                pltpu.SemaphoreType.DMA((4,)),
                pltpu.SemaphoreType.DMA((8,)),
            ],
        ),
        compiler_params=pltpu.CompilerParams(vmem_limit_bytes=60 << 20),
        cost_estimate=pl.CostEstimate(
            flops=2 * rows * columns * 2 * HDIM, transcendentals=0, bytes_accessed=15 << 20
        ),
    )(place, *attended, cotangent)


def on_device(
    queries, key_rows, value_rows, query_tangent, key_tangent, value_tangent, partners, cotangent
):
    own = to_heads(packed(key_rows, key_tangent, value_rows, value_tangent))
    halo = lax.ppermute(own[16:], "x", [(i, (i + 1) % 4) for i in range(4)])
    query, columns = lax.optimization_barrier((packed(query_tangent, queries), turned(cotangent)))
    query = to_heads(query)

    plane = lax.axis_index("x") * 4
    mine = lax.dynamic_slice_in_dim(partners, plane, 4, 0)
    near = (mine - plane + 2) % 16
    slots = jnp.concatenate([jnp.arange(2, 6, dtype=jnp.int32)[:, None], near], axis=1)
    late, sent = attend(slots[2:] - 2, query, (own,), ((0, 0, 0, 4),), True, 0, 2)
    window = ((1, 0, 0, 2), (0, 0, 2, 2))
    early1, sent = attend(slots[:2], query, (own, halo), window, False, 0, 1, sent)
    early2, sent = attend(slots[:2], query, (own, halo), window, False, 1, 1, sent)

    got_late = lax.ppermute(late, "zl", [(0, 1)])
    got1 = lax.ppermute(early1, "zl", [(1, 0)])
    last, *_ = lax.optimization_barrier((early2, got_late, got1))
    got2 = lax.ppermute(last, "zl", [(1, 0)])
    sent, _ = lax.optimization_barrier((sent, got2))
    back = lax.all_to_all(sent, PLANE, 0, 0, tiled=True)
    place = jnp.stack([lax.axis_index("x"), lax.axis_index("zl")]).astype(jnp.int32)
    terms = grad_terms(
        place, (early1, early2, got1, got2, late, got_late), columns
    )
    weight_grad = 0.0
    for n, term in enumerate(terms):
        dx, dz = HOPS[n // 2], n % 2
        if (dx, dz) != (0, 0):
            ring = [(2 * x + z, 2 * ((x + dx) % 4) + (z ^ dz)) for x in range(4) for z in range(2)]
            term = lax.ppermute(term, CLIPS, ring)
        weight_grad += term.astype(f32)
    attended, attended_tangent = unpack(back)
    return attended, attended_tangent, weight_grad


def solution(mesh):
    fine = Mesh(np.asarray(mesh.devices).reshape(4, 2, 2, 4, 2), EVERY)
    rows = P(EVERY, None)
    return jax.shard_map(
        on_device,
        mesh=fine,
        in_specs=(rows, rows, rows, rows, rows, rows, P(), P(CLIPS, None)),
        out_specs=(rows, rows, P(CLIPS, GROUP)),
        check_vma=False,
    )
```

```python
import functools

import jax
import jax.numpy as jnp
import numpy as np
from jax import lax
from jax.experimental import pallas as pl
from jax.experimental.pallas import tpu as pltpu
from jax.sharding import Mesh
from jax.sharding import PartitionSpec as P

HDIM = 128
CLIP = 1024
HEADS = 32
HALF = 64
SENDERS = 8
BLOCK = SENDERS * HALF
TILE = 256
HOPS = (2, 1, 3, 0)
LOG2E = 1.4426950408889634
PLANE = ("zl", "zh", "y", "c")
GROUP = ("zh", "y", "c")
CLIPS = ("x", "zl")
EVERY = ("x", "zl", "zh", "y", "c")
NT = (((1,), (1,)), ((), ()))
bf16, f32 = jnp.bfloat16, jnp.float32


def pack_kernel(*refs):
    count = len(refs) - 5
    ins, (out, rows, cut, arrived, left) = refs[:count], refs[count:]
    steps = arrived.shape[0]
    heads = HEADS // steps
    width = heads * HDIM
    reads = [
        [
            pltpu.make_async_copy(
                ref.at[:, pl.ds(step * width, width)],
                rows.at[n, :, pl.ds(step * width, width)],
                arrived.at[step, n],
            )
            for n, ref in enumerate(ins)
        ]
        for step in range(steps)
    ]
    for copies in reads:
        for copy in copies:
            copy.start()
    writes = []
    for step, copies in enumerate(reads):
        for n, copy in enumerate(copies):
            copy.wait()
            for head in range(step * heads, (step + 1) * heads):
                cut[head % 2, head // 2, :, n * HDIM : (n + 1) * HDIM] = rows[
                    n, :, head * HDIM : (head + 1) * HDIM
                ]
        part = pl.ds(step * heads // 2, heads // 2)
        writes.append(pltpu.make_async_copy(cut.at[:, part], out.at[:, part], left.at[step]))
        writes[-1].start()
    for copy in writes:
        copy.wait()


def packed(*arrays):
    count = len(arrays)
    rows, width = arrays[0].shape[0], count * HDIM
    steps = 4
    anywhere = pl.BlockSpec(memory_space=pl.ANY)
    return pl.pallas_call(
        pack_kernel,
        out_shape=jax.ShapeDtypeStruct((2, 16, rows, width), bf16),
        in_specs=[anywhere] * count,
        out_specs=anywhere,
        scratch_shapes=[
            pltpu.VMEM((count, rows, HEADS * HDIM), bf16),
            pltpu.VMEM((2, 16, rows, width), bf16),
            pltpu.SemaphoreType.DMA((steps, count)),
            pltpu.SemaphoreType.DMA((steps,)),
        ],
        compiler_params=pltpu.CompilerParams(vmem_limit_bytes=60 << 20),
        cost_estimate=pl.CostEstimate(
            flops=0, transcendentals=0, bytes_accessed=4 * rows * HEADS * width
        ),
    )(*arrays).reshape(32, rows, width)


def to_heads(sent):
    return lax.all_to_all(sent, PLANE, 0, 0, tiled=True)


def unpack_kernel(ref, out_ref, tan_ref):
    for head in range(8):
        lanes = slice(head * HDIM, (head + 1) * HDIM)
        out_ref[:, lanes] = ref[head % 2, head // 2, :, :HDIM]
        tan_ref[:, lanes] = ref[head % 2, head // 2, :, HDIM:]


def unpack(back):
    rows = back.shape[1]
    shape = jax.ShapeDtypeStruct((rows, HEADS * HDIM), bf16)
    spec = pl.BlockSpec((rows, 8 * HDIM), lambda j: (0, j))
    return pl.pallas_call(
        unpack_kernel,
        out_shape=(shape, shape),
        grid=(4,),
        in_specs=[pl.BlockSpec((2, 4, rows, 2 * HDIM), lambda j: (0, j, 0, 0))],
        out_specs=(spec, spec),
        cost_estimate=pl.CostEstimate(flops=0, transcendentals=0, bytes_accessed=4 << 20),
    )(back.reshape(2, 16, rows, 2 * HDIM))


def attend_kernel(slots_ref, q_ref, *rest, loads, sources, halves, first, first_half):
    kept, rest = rest[:sources], rest[sources:]
    *outs, queries, kv, scores, tangents, sem, query_sem = rest
    scale = HDIM**-0.5
    half, clip = pl.program_id(0), pl.program_id(1)
    start = (half == 0) & (clip == 0)
    split = 2 * HDIM
    blocks = [(h, c) for h in range(halves) for c in range(2)]

    def fetch(step, at):
        return pltpu.make_async_copy(
            q_ref.at[
                pl.ds((first + at[1]) * SENDERS, SENDERS),
                pl.ds((first_half + at[0]) * HALF, HALF),
            ],
            queries.at[step],
            query_sem.at[step],
        )

    def copies(part):
        lanes = pl.ds(part * split, split)
        return [
            pltpu.make_async_copy(
                kept[which].at[pl.ds(source * SENDERS, count * SENDERS), :, lanes],
                kv.at[pl.ds(target * SENDERS, count * SENDERS), :, lanes],
                sem.at[part, n],
            )
            for n, (which, source, target, count) in enumerate(loads)
        ]

    @pl.when(start)
    def _():
        fetches = [fetch(step, at) for step, at in enumerate(blocks)]
        for copy in copies(0) + fetches:
            copy.start()
        for copy in copies(0) + fetches:
            copy.wait()
        for copy in copies(1):
            copy.start()

    both = queries[2 * half + clip].reshape(BLOCK, 2 * HDIM)
    query = both[:, HDIM:]
    picks = [slots_ref[clip, n] * SENDERS for n in range(3)]
    tiles = [(n, k) for n in range(3) for k in range(0, CLIP, TILE)]

    def window(n, k, lanes):
        rows = pl.ds(picks[n] + k // 128, TILE // 128)
        return kv[rows, :, lanes].reshape(TILE, -1)

    top = None
    for n, k in tiles:
        part = lax.dot_general(query, window(n, k, slice(0, HDIM)), NT, preferred_element_type=f32)
        at = n * CLIP + k
        scores[:, at : at + TILE] = part
        for lane in range(0, TILE, HDIM):
            piece = part[:, lane : lane + HDIM]
            top = piece if top is None else jnp.maximum(top, piece)
    top = jnp.broadcast_to(jnp.max(top, axis=1, keepdims=True), (BLOCK, HDIM))
    total = jnp.zeros((BLOCK, HDIM), f32)
    mean = jnp.zeros((BLOCK, HDIM), f32)
    for n, k in tiles:
        tangent = lax.dot_general(
            both, window(n, k, slice(0, 2 * HDIM)), NT, preferred_element_type=f32
        )
        for lane in range(0, TILE, HDIM):
            at = n * CLIP + k + lane
            part = jnp.exp2((scores[:, at : at + HDIM] - top) * (scale * LOG2E))
            moved = part * tangent[:, lane : lane + HDIM]
            total += part
            mean += moved
            scores[:, at : at + HDIM] = part
            tangents[:, at : at + HDIM] = moved
    inverse = 1.0 / jnp.sum(total, axis=1, keepdims=True)
    mean = jnp.broadcast_to(jnp.sum(mean, axis=1, keepdims=True) * inverse, (BLOCK, HDIM))

    @pl.when(start)
    def _():
        for copy in copies(1):
            copy.wait()

    out = jnp.zeros((BLOCK, 2 * HDIM), f32)
    tan = jnp.zeros((BLOCK, HDIM), f32)
    for n, k in tiles:
        weights, weights_tan = [], []
        for lane in range(0, TILE, HDIM):
            at = n * CLIP + k + lane
            part = scores[:, at : at + HDIM]
            weights.append(part.astype(bf16))
            weights_tan.append((tangents[:, at : at + HDIM] - part * mean).astype(bf16))
        out += jnp.dot(
            jnp.concatenate(weights, axis=1),
            window(n, k, slice(2 * HDIM, 4 * HDIM)),
            preferred_element_type=f32,
        )
        tan += jnp.dot(
            jnp.concatenate(weights_tan, axis=1),
            window(n, k, slice(2 * HDIM, 3 * HDIM)),
            preferred_element_type=f32,
        )
    result = (out[:, :HDIM] * inverse).astype(bf16).reshape(SENDERS, HALF, HDIM)
    result_tan = ((tan * scale + out[:, HDIM:]) * inverse).astype(bf16)
    result_tan = result_tan.reshape(SENDERS, HALF, HDIM)

    pair_ref, sent_ref = outs
    pair_ref[0] = result
    sent_ref[:, :, :HDIM] = result
    sent_ref[:, :, HDIM:] = result_tan


def attend(slots, queries, kept, loads, late, first_half, halves, filled=None):
    first = 2 if late else 0
    in_specs = [pl.BlockSpec(memory_space=pl.ANY)] * (1 + len(kept) + (filled is not None))
    out_shape = (
        jax.ShapeDtypeStruct((halves, 16, HALF, HDIM), bf16),
        jax.ShapeDtypeStruct((32, 2 * HALF, 2 * HDIM), bf16),
    )
    out_specs = (
        pl.BlockSpec((1, SENDERS, HALF, HDIM), lambda h, c, s: (h, c, 0, 0)),
        pl.BlockSpec(
            (SENDERS, HALF, 2 * HDIM), lambda h, c, s: (first + c, first_half + h, 0)
        ),
    )
    operands = (slots, queries, *kept) + (() if filled is None else (filled,))
    return pl.pallas_call(
        functools.partial(
            attend_kernel,
            loads=loads,
            sources=len(kept) + (filled is not None),
            halves=halves,
            first=first,
            first_half=first_half,
        ),
        out_shape=out_shape,
        grid_spec=pltpu.PrefetchScalarGridSpec(
            num_scalar_prefetch=1,
            grid=(halves, 2),
            in_specs=in_specs,
            out_specs=out_specs,
            scratch_shapes=[
                pltpu.VMEM((2 * halves, SENDERS, HALF, 2 * HDIM), bf16),
                pltpu.VMEM((4 * SENDERS, 128, 4 * HDIM), bf16),
                pltpu.VMEM((BLOCK, 3 * CLIP), f32),
                pltpu.VMEM((BLOCK, 3 * CLIP), f32),
                pltpu.SemaphoreType.DMA((2, len(loads))),
                pltpu.SemaphoreType.DMA((2 * halves,)),
            ],
        ),
        input_output_aliases={} if filled is None else {len(operands) - 1: 1},
        compiler_params=pltpu.CompilerParams(
            dimension_semantics=("arbitrary", "arbitrary"), vmem_limit_bytes=28 << 20
        ),
        cost_estimate=pl.CostEstimate(
            flops=2 * 2 * halves * BLOCK * 3 * CLIP * HDIM * 8,
            transcendentals=2 * halves * BLOCK * 3 * CLIP,
            bytes_accessed=8 << 20,
        ),
    )(*operands)


def turn_kernel(ref, out_ref):
    out_ref[...] = ref[...].T


def turned(cotangent):
    rows, columns = cotangent.shape
    return pl.pallas_call(
        turn_kernel,
        out_shape=jax.ShapeDtypeStruct((columns, rows), bf16),
        grid=(8,),
        in_specs=[pl.BlockSpec((rows, columns // 8), lambda j: (0, j))],
        out_specs=pl.BlockSpec((columns // 8, rows), lambda j: (j, 0)),
        compiler_params=pltpu.CompilerParams(vmem_limit_bytes=32 << 20),
        cost_estimate=pl.CostEstimate(flops=0, transcendentals=0, bytes_accessed=24 << 20),
    )(cotangent)


def grad_kernel(place_ref, early_a, early_b, got_a, got_b, late, got_late, cot_ref, *rest):
    outs, (pair, rows, parts, sem, arrived, left) = rest[:8], rest[8:]
    plane, side = place_ref[0], place_ref[1]
    height = 2 * parts.shape[2]
    reads = [
        pltpu.make_async_copy(
            cot_ref.at[pl.ds(pl.multiple_of((plane + dx) % 4 * height, height), height)],
            rows.at[step],
            arrived.at[step],
        )
        for step, dx in enumerate(HOPS)
    ]
    reads[0].start()
    reads[1].start()

    def load(left_halves, right_halves):
        copies = []
        for column, halves in enumerate((left_halves, right_halves)):
            for half, ref in enumerate(halves):
                copies.append(
                    pltpu.make_async_copy(
                        ref,
                        pair.at[:, pl.ds(half * HALF, HALF), pl.ds(column * HDIM, HDIM)],
                        sem.at[2 * column + half],
                    )
                )
        for copy in copies:
            copy.start()
        for copy in copies:
            copy.wait()

    halves = lambda ref: (ref.at[0], ref.at[1])
    own = (early_a.at[0], early_b.at[0])
    far = (got_a.at[0], got_b.at[0])
    pl.when(side == 0)(lambda: load(own, far))
    pl.when(side == 1)(lambda: load(halves(got_late), halves(late)))
    writes = []
    for step, copy in enumerate(reads):
        copy.wait()
        if step + 2 < len(reads):
            reads[step + 2].start()
        part = jnp.dot(
            rows[step], pair[...].reshape(2 * CLIP, 2 * HDIM), preferred_element_type=f32
        )
        parts[step] = part.astype(bf16).reshape(2, height // 2, 2 * HDIM)
        for dz in range(2):
            n = 2 * step + dz
            writes.append(
                pltpu.make_async_copy(parts.at[step, side ^ dz], outs[n], left.at[n])
            )
            writes[-1].start()
    for copy in writes:
        copy.wait()


def grad_terms(place, attended, cotangent):
    columns, rows = cotangent.shape
    width = columns // 8
    anywhere = pl.BlockSpec(memory_space=pl.ANY)
    return pl.pallas_call(
        grad_kernel,
        out_shape=[jax.ShapeDtypeStruct((width, 2 * HDIM), bf16)] * 8,
        grid_spec=pltpu.PrefetchScalarGridSpec(
            num_scalar_prefetch=1,
            grid=(),
            in_specs=[anywhere] * 7,
            out_specs=[anywhere] * 8,
            scratch_shapes=[
                pltpu.VMEM((16, 2 * HALF, 2 * HDIM), bf16),
                pltpu.VMEM((4, 2 * width, rows), bf16),
                pltpu.VMEM((4, 2, width, 2 * HDIM), bf16),
                pltpu.SemaphoreType.DMA((4,)),
                pltpu.SemaphoreType.DMA((4,)),
                pltpu.SemaphoreType.DMA((8,)),
            ],
        ),
        compiler_params=pltpu.CompilerParams(vmem_limit_bytes=56 << 20),
        cost_estimate=pl.CostEstimate(
            flops=2 * rows * columns * 2 * HDIM, transcendentals=0, bytes_accessed=15 << 20
        ),
    )(place, *attended, cotangent)


def on_device(
    queries, key_rows, value_rows, query_tangent, key_tangent, value_tangent, partners, cotangent
):
    own = to_heads(packed(key_rows, key_tangent, value_rows, value_tangent))
    halo = lax.ppermute(own[16:], "x", [(i, (i + 1) % 4) for i in range(4)])
    query, columns = lax.optimization_barrier((packed(query_tangent, queries), turned(cotangent)))
    query = to_heads(query)

    plane = lax.axis_index("x") * 4
    mine = lax.dynamic_slice_in_dim(partners, plane, 4, 0)
    near = (mine - plane + 2) % 16
    slots = jnp.concatenate([jnp.arange(2, 6, dtype=jnp.int32)[:, None], near], axis=1)
    late, sent = attend(slots[2:] - 2, query, (own,), ((0, 0, 0, 4),), True, 0, 2)
    window = ((1, 0, 0, 2), (0, 0, 2, 2))
    early1, sent = attend(slots[:2], query, (own, halo), window, False, 0, 1, sent)
    early2, sent = attend(slots[:2], query, (own, halo), window, False, 1, 1, sent)

    got_late = lax.ppermute(late, "zl", [(0, 1)])
    got1 = lax.ppermute(early1, "zl", [(1, 0)])
    last, *_ = lax.optimization_barrier((early2, got_late, got1))
    got2 = lax.ppermute(last, "zl", [(1, 0)])
    sent, _ = lax.optimization_barrier((sent, got2))
    back = lax.all_to_all(sent, PLANE, 0, 0, tiled=True)
    place = jnp.stack([lax.axis_index("x"), lax.axis_index("zl")]).astype(jnp.int32)
    terms = grad_terms(
        place, (early1, early2, got1, got2, late, got_late), columns
    )
    arrived = []
    for n, term in enumerate(terms):
        dx, dz = HOPS[n // 2], n % 2
        ring = [(2 * x + z, 2 * ((x + dx) % 4) + (z ^ dz)) for x in range(4) for z in range(2)]
        arrived.append(term if (dx, dz) == (0, 0) else lax.ppermute(term, CLIPS, ring))
    rows, arrived = lax.optimization_barrier((unpack(back), arrived))
    weight_grad = sum(term.astype(f32) for term in arrived)
    return *rows, weight_grad


def solution(mesh):
    fine = Mesh(np.asarray(mesh.devices).reshape(4, 2, 2, 4, 2), EVERY)
    rows = P(EVERY, None)
    return jax.shard_map(
        on_device,
        mesh=fine,
        in_specs=(rows, rows, rows, rows, rows, rows, P(), P(CLIPS, None)),
        out_specs=(rows, rows, P(CLIPS, GROUP)),
        check_vma=False,
    )
```

```python
import functools

import jax
import jax.numpy as jnp
import numpy as np
from jax import lax
from jax.experimental import pallas as pl
from jax.experimental.pallas import tpu as pltpu
from jax.sharding import Mesh
from jax.sharding import PartitionSpec as P

HDIM = 128
CLIP = 1024
HEADS = 32
HALF = 64
SENDERS = 8
BLOCK = SENDERS * HALF
TILE = 256
HOPS = (2, 1, 3, 0)
LOG2E = 1.4426950408889634
PLANE = ("zl", "zh", "y", "c")
GROUP = ("zh", "y", "c")
CLIPS = ("x", "zl")
EVERY = ("x", "zl", "zh", "y", "c")
NT = (((1,), (1,)), ((), ()))
bf16, f32 = jnp.bfloat16, jnp.float32


def pack_kernel(*refs):
    count = len(refs) - 5
    ins, (out, rows, cut, arrived, left) = refs[:count], refs[count:]
    steps = arrived.shape[0]
    heads = HEADS // steps
    width = heads * HDIM
    reads = [
        [
            pltpu.make_async_copy(
                ref.at[:, pl.ds(step * width, width)],
                rows.at[n, :, pl.ds(step * width, width)],
                arrived.at[step, n],
            )
            for n, ref in enumerate(ins)
        ]
        for step in range(steps)
    ]
    for copies in reads:
        for copy in copies:
            copy.start()
    writes = []
    for step, copies in enumerate(reads):
        for n, copy in enumerate(copies):
            copy.wait()
            for head in range(step * heads, (step + 1) * heads):
                cut[head % 2, head // 2, :, n * HDIM : (n + 1) * HDIM] = rows[
                    n, :, head * HDIM : (head + 1) * HDIM
                ]
        part = pl.ds(step * heads // 2, heads // 2)
        writes.append(pltpu.make_async_copy(cut.at[:, part], out.at[:, part], left.at[step]))
        writes[-1].start()
    for copy in writes:
        copy.wait()


def packed(*arrays):
    count = len(arrays)
    rows, width = arrays[0].shape[0], count * HDIM
    steps = 4
    anywhere = pl.BlockSpec(memory_space=pl.ANY)
    return pl.pallas_call(
        pack_kernel,
        out_shape=jax.ShapeDtypeStruct((2, 16, rows, width), bf16),
        in_specs=[anywhere] * count,
        out_specs=anywhere,
        scratch_shapes=[
            pltpu.VMEM((count, rows, HEADS * HDIM), bf16),
            pltpu.VMEM((2, 16, rows, width), bf16),
            pltpu.SemaphoreType.DMA((steps, count)),
            pltpu.SemaphoreType.DMA((steps,)),
        ],
        compiler_params=pltpu.CompilerParams(vmem_limit_bytes=60 << 20),
        cost_estimate=pl.CostEstimate(
            flops=0, transcendentals=0, bytes_accessed=4 * rows * HEADS * width
        ),
    )(*arrays).reshape(32, rows, width)


def to_heads(sent):
    return lax.all_to_all(sent, PLANE, 0, 0, tiled=True)


def unpack_kernel(even_ref, odd_ref, out_ref, tan_ref):
    for head in range(8):
        lanes = slice(head * HDIM, (head + 1) * HDIM)
        ref = odd_ref if head % 2 else even_ref
        out_ref[:, lanes] = ref[head // 2, :, :HDIM]
        tan_ref[:, lanes] = ref[head // 2, :, HDIM:]


def unpack(back):
    rows = back.shape[1]
    shape = jax.ShapeDtypeStruct((rows, HEADS * HDIM), bf16)
    spec = pl.BlockSpec((rows, 8 * HDIM), lambda j: (0, j))
    return pl.pallas_call(
        unpack_kernel,
        out_shape=(shape, shape),
        grid=(4,),
        in_specs=[
            pl.BlockSpec((4, rows, 2 * HDIM), lambda j: (j, 0, 0)),
            pl.BlockSpec((4, rows, 2 * HDIM), lambda j: (4 + j, 0, 0)),
        ],
        out_specs=(spec, spec),
        cost_estimate=pl.CostEstimate(flops=0, transcendentals=0, bytes_accessed=4 << 20),
    )(back, back)


def attend_kernel(slots_ref, q_ref, *rest, loads, sources, halves, first, first_half):
    kept, rest = rest[:sources], rest[sources:]
    *outs, queries, kv, scores, tangents, sem, query_sem = rest
    scale = HDIM**-0.5
    half, clip = pl.program_id(0), pl.program_id(1)
    start = (half == 0) & (clip == 0)
    split = 2 * HDIM
    blocks = [(h, c) for h in range(halves) for c in range(2)]

    def fetch(step, at):
        return pltpu.make_async_copy(
            q_ref.at[
                pl.ds((first + at[1]) * SENDERS, SENDERS),
                pl.ds((first_half + at[0]) * HALF, HALF),
            ],
            queries.at[step],
            query_sem.at[step],
        )

    def copies(part):
        lanes = pl.ds(part * split, split)
        return [
            pltpu.make_async_copy(
                kept[which].at[pl.ds(source * SENDERS, count * SENDERS), :, lanes],
                kv.at[pl.ds(target * SENDERS, count * SENDERS), :, lanes],
                sem.at[part, n],
            )
            for n, (which, source, target, count) in enumerate(loads)
        ]

    @pl.when(start)
    def _():
        fetches = [fetch(step, at) for step, at in enumerate(blocks)]
        for copy in copies(0) + fetches:
            copy.start()
        for copy in copies(0) + fetches:
            copy.wait()
        for copy in copies(1):
            copy.start()

    both = queries[2 * half + clip].reshape(BLOCK, 2 * HDIM)
    query = both[:, HDIM:]
    picks = [slots_ref[clip, n] * SENDERS for n in range(3)]
    tiles = [(n, k) for n in range(3) for k in range(0, CLIP, TILE)]

    def window(n, k, lanes):
        rows = pl.ds(picks[n] + k // 128, TILE // 128)
        return kv[rows, :, lanes].reshape(TILE, -1)

    top = None
    for n, k in tiles:
        part = lax.dot_general(query, window(n, k, slice(0, HDIM)), NT, preferred_element_type=f32)
        at = n * CLIP + k
        scores[:, at : at + TILE] = part
        for lane in range(0, TILE, HDIM):
            piece = part[:, lane : lane + HDIM]
            top = piece if top is None else jnp.maximum(top, piece)
    top = jnp.broadcast_to(jnp.max(top, axis=1, keepdims=True), (BLOCK, HDIM))
    total = jnp.zeros((BLOCK, HDIM), f32)
    mean = jnp.zeros((BLOCK, HDIM), f32)
    for n, k in tiles:
        tangent = lax.dot_general(
            both, window(n, k, slice(0, 2 * HDIM)), NT, preferred_element_type=f32
        )
        for lane in range(0, TILE, HDIM):
            at = n * CLIP + k + lane
            part = jnp.exp2((scores[:, at : at + HDIM] - top) * (scale * LOG2E))
            moved = part * tangent[:, lane : lane + HDIM]
            total += part
            mean += moved
            scores[:, at : at + HDIM] = part
            tangents[:, at : at + HDIM] = moved
    inverse = 1.0 / jnp.sum(total, axis=1, keepdims=True)
    mean = jnp.broadcast_to(jnp.sum(mean, axis=1, keepdims=True) * inverse, (BLOCK, HDIM))

    @pl.when(start)
    def _():
        for copy in copies(1):
            copy.wait()

    out = jnp.zeros((BLOCK, 2 * HDIM), f32)
    tan = jnp.zeros((BLOCK, HDIM), f32)
    for n, k in tiles:
        weights, weights_tan = [], []
        for lane in range(0, TILE, HDIM):
            at = n * CLIP + k + lane
            part = scores[:, at : at + HDIM]
            weights.append(part.astype(bf16))
            weights_tan.append((tangents[:, at : at + HDIM] - part * mean).astype(bf16))
        out += jnp.dot(
            jnp.concatenate(weights, axis=1),
            window(n, k, slice(2 * HDIM, 4 * HDIM)),
            preferred_element_type=f32,
        )
        tan += jnp.dot(
            jnp.concatenate(weights_tan, axis=1),
            window(n, k, slice(2 * HDIM, 3 * HDIM)),
            preferred_element_type=f32,
        )
    result = (out[:, :HDIM] * inverse).astype(bf16).reshape(SENDERS, HALF, HDIM)
    result_tan = ((tan * scale + out[:, HDIM:]) * inverse).astype(bf16)
    result_tan = result_tan.reshape(SENDERS, HALF, HDIM)

    pair_ref, sent_ref = outs
    pair_ref[0] = result
    sent_ref[:, :, :HDIM] = result
    sent_ref[:, :, HDIM:] = result_tan


def attend(slots, queries, kept, loads, late, first_half, halves, filled=None):
    first = 2 if late else 0
    in_specs = [pl.BlockSpec(memory_space=pl.ANY)] * (1 + len(kept) + (filled is not None))
    out_shape = (
        jax.ShapeDtypeStruct((halves, 16, HALF, HDIM), bf16),
        jax.ShapeDtypeStruct((32, 2 * HALF, 2 * HDIM), bf16),
    )
    out_specs = (
        pl.BlockSpec((1, SENDERS, HALF, HDIM), lambda h, c, s: (h, c, 0, 0)),
        pl.BlockSpec(
            (SENDERS, HALF, 2 * HDIM), lambda h, c, s: (first + c, first_half + h, 0)
        ),
    )
    operands = (slots, queries, *kept) + (() if filled is None else (filled,))
    return pl.pallas_call(
        functools.partial(
            attend_kernel,
            loads=loads,
            sources=len(kept) + (filled is not None),
            halves=halves,
            first=first,
            first_half=first_half,
        ),
        out_shape=out_shape,
        grid_spec=pltpu.PrefetchScalarGridSpec(
            num_scalar_prefetch=1,
            grid=(halves, 2),
            in_specs=in_specs,
            out_specs=out_specs,
            scratch_shapes=[
                pltpu.VMEM((2 * halves, SENDERS, HALF, 2 * HDIM), bf16),
                pltpu.VMEM((4 * SENDERS, 128, 4 * HDIM), bf16),
                pltpu.VMEM((BLOCK, 3 * CLIP), f32),
                pltpu.VMEM((BLOCK, 3 * CLIP), f32),
                pltpu.SemaphoreType.DMA((2, len(loads))),
                pltpu.SemaphoreType.DMA((2 * halves,)),
            ],
        ),
        input_output_aliases={} if filled is None else {len(operands) - 1: 1},
        compiler_params=pltpu.CompilerParams(
            dimension_semantics=("arbitrary", "arbitrary"), vmem_limit_bytes=28 << 20
        ),
        cost_estimate=pl.CostEstimate(
            flops=2 * 2 * halves * BLOCK * 3 * CLIP * HDIM * 8,
            transcendentals=2 * halves * BLOCK * 3 * CLIP,
            bytes_accessed=8 << 20,
        ),
    )(*operands)


def turn_kernel(ref, out_ref):
    out_ref[...] = ref[...].T


def turned(cotangent):
    rows, columns = cotangent.shape
    return pl.pallas_call(
        turn_kernel,
        out_shape=jax.ShapeDtypeStruct((columns, rows), bf16),
        grid=(8,),
        in_specs=[pl.BlockSpec((rows, columns // 8), lambda j: (0, j))],
        out_specs=pl.BlockSpec((columns // 8, rows), lambda j: (j, 0)),
        compiler_params=pltpu.CompilerParams(vmem_limit_bytes=32 << 20),
        cost_estimate=pl.CostEstimate(flops=0, transcendentals=0, bytes_accessed=24 << 20),
    )(cotangent)


def grad_kernel(place_ref, early_a, early_b, late_a, late_b, cot_ref, *rest, both):
    if both:
        other, rest = rest[0], rest[1:]
    outs, (tokens, rows, parts, sem, arrived, left) = rest[:-6], rest[-6:]
    plane, side = place_ref[0], place_ref[1]
    height = 2 * parts.shape[2]
    first = slice(0, HDIM)
    mine = slice(HDIM, 2 * HDIM) if both else first
    reads = [
        pltpu.make_async_copy(
            cot_ref.at[pl.ds(pl.multiple_of((plane + dx) % 4 * height, height), height)],
            rows.at[step],
            arrived.at[step],
        )
        for step, dx in enumerate(HOPS)
    ]

    def load(halves):
        copies = [
            pltpu.make_async_copy(ref, tokens.at[:, pl.ds(n * HALF, HALF)], sem.at[n])
            for n, ref in enumerate(halves)
        ]
        for copy in copies:
            copy.start()
        for copy in copies:
            copy.wait()

    reads[0].start()
    reads[1].start()
    pl.when(side == 0)(lambda: load((early_a.at[0], early_b.at[0])))
    pl.when(side == 1)(lambda: load((late_a.at[0], late_b.at[1])))
    if both:
        fill = pltpu.make_async_copy(other, parts.at[:, :, :, pl.ds(0, HDIM)], sem.at[0])
        fill.start()
    writes = []
    for step, copy in enumerate(reads):
        copy.wait()
        if step + 2 < len(reads):
            reads[step + 2].start()
        part = jnp.dot(
            rows[step], tokens[...].reshape(2 * CLIP, HDIM), preferred_element_type=f32
        )
        parts[step, :, :, mine] = part.astype(bf16).reshape(2, height // 2, HDIM)
        if both:
            if step == 0:
                fill.wait()
            for dz in range(2):
                n = 2 * step + dz
                writes.append(
                    pltpu.make_async_copy(parts.at[step, side ^ dz], outs[n], left.at[n])
                )
                writes[-1].start()
        else:
            writes.append(pltpu.make_async_copy(parts.at[step], outs[0].at[step], left.at[step]))
            writes[-1].start()
    for copy in writes:
        copy.wait()


def grad_terms(place, attended, cotangent, other=None):
    columns, rows = cotangent.shape
    width = columns // 8
    anywhere = pl.BlockSpec(memory_space=pl.ANY)
    both = other is not None
    held = (2 if both else 1) * HDIM
    if both:
        out_shape = [jax.ShapeDtypeStruct((width, held), bf16)] * 8
    else:
        out_shape = [jax.ShapeDtypeStruct((4, 2, width, held), bf16)]
    operands = (*attended, cotangent) + ((other,) if both else ())
    return pl.pallas_call(
        functools.partial(grad_kernel, both=both),
        out_shape=out_shape,
        grid_spec=pltpu.PrefetchScalarGridSpec(
            num_scalar_prefetch=1,
            grid=(),
            in_specs=[anywhere] * len(operands),
            out_specs=[anywhere] * len(out_shape),
            scratch_shapes=[
                pltpu.VMEM((16, 2 * HALF, HDIM), bf16),
                pltpu.VMEM((4, 2 * width, rows), bf16),
                pltpu.VMEM((4, 2, width, held), bf16),
                pltpu.SemaphoreType.DMA((2,)),
                pltpu.SemaphoreType.DMA((4,)),
                pltpu.SemaphoreType.DMA((8,)),
            ],
        ),
        compiler_params=pltpu.CompilerParams(vmem_limit_bytes=50 << 20),
        cost_estimate=pl.CostEstimate(
            flops=2 * rows * columns * 2 * HDIM, transcendentals=0, bytes_accessed=15 << 20
        ),
    )(place, *operands)


def on_device(
    queries, key_rows, value_rows, query_tangent, key_tangent, value_tangent, partners, cotangent
):
    own = to_heads(packed(key_rows, key_tangent, value_rows, value_tangent))
    halo = lax.ppermute(own[16:], "x", [(i, (i + 1) % 4) for i in range(4)])
    query, columns = lax.optimization_barrier((packed(query_tangent, queries), turned(cotangent)))
    query = to_heads(query)

    plane = lax.axis_index("x") * 4
    mine = lax.dynamic_slice_in_dim(partners, plane, 4, 0)
    near = (mine - plane + 2) % 16
    slots = jnp.concatenate([jnp.arange(2, 6, dtype=jnp.int32)[:, None], near], axis=1)
    late, sent = attend(slots[2:] - 2, query, (own,), ((0, 0, 0, 4),), True, 0, 2)
    window = ((1, 0, 0, 2), (0, 0, 2, 2))
    early1, sent = attend(slots[:2], query, (own, halo), window, False, 0, 1, sent)
    early2, sent = attend(slots[:2], query, (own, halo), window, False, 1, 1, sent)

    got_late = lax.ppermute(late, "zl", [(0, 1)])
    got1 = lax.ppermute(early1, "zl", [(1, 0)])
    last, *_ = lax.optimization_barrier((early2, got_late, got1))
    got2 = lax.ppermute(last, "zl", [(1, 0)])
    place = jnp.stack([lax.axis_index("x"), lax.axis_index("zl")]).astype(jnp.int32)
    first_columns = grad_terms(place, (early1, early2, got_late, got_late), columns)
    sent, first_columns, _ = lax.optimization_barrier((sent, first_columns, got2))
    back = lax.all_to_all(sent, PLANE, 0, 0, tiled=True)
    terms = grad_terms(place, (got1, got2, late, late), columns, *first_columns)
    arrived = []
    for n, term in enumerate(terms):
        dx, dz = HOPS[n // 2], n % 2
        ring = [(2 * x + z, 2 * ((x + dx) % 4) + (z ^ dz)) for x in range(4) for z in range(2)]
        arrived.append(term if (dx, dz) == (0, 0) else lax.ppermute(term, CLIPS, ring))
    weight_grad = sum(term.astype(f32) for term in arrived)
    return *unpack(back), weight_grad


def solution(mesh):
    fine = Mesh(np.asarray(mesh.devices).reshape(4, 2, 2, 4, 2), EVERY)
    rows = P(EVERY, None)
    return jax.shard_map(
        on_device,
        mesh=fine,
        in_specs=(rows, rows, rows, rows, rows, rows, P(), P(CLIPS, None)),
        out_specs=(rows, rows, P(CLIPS, GROUP)),
        check_vma=False,
    )
```

```python
import functools

import jax
import jax.numpy as jnp
import numpy as np
from jax import lax
from jax.experimental import pallas as pl
from jax.experimental.pallas import tpu as pltpu
from jax.sharding import Mesh
from jax.sharding import PartitionSpec as P

HDIM = 128
CLIP = 1024
HEADS = 32
HALF = 64
SENDERS = 8
BLOCK = SENDERS * HALF
TILE = 256
HOPS = (2, 1, 3, 0)
LOG2E = 1.4426950408889634
PLANE = ("zl", "zh", "y", "c")
GROUP = ("zh", "y", "c")
CLIPS = ("x", "zl")
EVERY = ("x", "zl", "zh", "y", "c")
NT = (((1,), (1,)), ((), ()))
bf16, f32 = jnp.bfloat16, jnp.float32


def pack_kernel(*refs):
    count = len(refs) - 5
    ins, (out, rows, cut, arrived, left) = refs[:count], refs[count:]
    steps = arrived.shape[0]
    heads = HEADS // steps
    width = heads * HDIM
    reads = [
        [
            pltpu.make_async_copy(
                ref.at[:, pl.ds(step * width, width)],
                rows.at[n, :, pl.ds(step * width, width)],
                arrived.at[step, n],
            )
            for n, ref in enumerate(ins)
        ]
        for step in range(steps)
    ]
    for copies in reads:
        for copy in copies:
            copy.start()
    writes = []
    for step, copies in enumerate(reads):
        for n, copy in enumerate(copies):
            copy.wait()
            for head in range(step * heads, (step + 1) * heads):
                cut[head % 2, head // 2, :, n * HDIM : (n + 1) * HDIM] = rows[
                    n, :, head * HDIM : (head + 1) * HDIM
                ]
        part = pl.ds(step * heads // 2, heads // 2)
        writes.append(pltpu.make_async_copy(cut.at[:, part], out.at[:, part], left.at[step]))
        writes[-1].start()
    for copy in writes:
        copy.wait()


def packed(*arrays):
    count = len(arrays)
    rows, width = arrays[0].shape[0], count * HDIM
    steps = 4
    anywhere = pl.BlockSpec(memory_space=pl.ANY)
    return pl.pallas_call(
        pack_kernel,
        out_shape=jax.ShapeDtypeStruct((2, 16, rows, width), bf16),
        in_specs=[anywhere] * count,
        out_specs=anywhere,
        scratch_shapes=[
            pltpu.VMEM((count, rows, HEADS * HDIM), bf16),
            pltpu.VMEM((2, 16, rows, width), bf16),
            pltpu.SemaphoreType.DMA((steps, count)),
            pltpu.SemaphoreType.DMA((steps,)),
        ],
        compiler_params=pltpu.CompilerParams(vmem_limit_bytes=60 << 20),
        cost_estimate=pl.CostEstimate(
            flops=0, transcendentals=0, bytes_accessed=4 * rows * HEADS * width
        ),
    )(*arrays).reshape(32, rows, width)


def to_heads(sent):
    return lax.all_to_all(sent, PLANE, 0, 0, tiled=True)


def unpack_kernel(even_ref, odd_ref, out_ref, tan_ref):
    for head in range(8):
        lanes = slice(head * HDIM, (head + 1) * HDIM)
        ref = odd_ref if head % 2 else even_ref
        out_ref[:, lanes] = ref[head // 2, :, :HDIM]
        tan_ref[:, lanes] = ref[head // 2, :, HDIM:]


def unpack(back):
    rows = back.shape[1]
    shape = jax.ShapeDtypeStruct((rows, HEADS * HDIM), bf16)
    spec = pl.BlockSpec((rows, 8 * HDIM), lambda j: (0, j))
    return pl.pallas_call(
        unpack_kernel,
        out_shape=(shape, shape),
        grid=(4,),
        in_specs=[
            pl.BlockSpec((4, rows, 2 * HDIM), lambda j: (j, 0, 0)),
            pl.BlockSpec((4, rows, 2 * HDIM), lambda j: (4 + j, 0, 0)),
        ],
        out_specs=(spec, spec),
        cost_estimate=pl.CostEstimate(flops=0, transcendentals=0, bytes_accessed=4 << 20),
    )(back, back)


def attend_kernel(slots_ref, q_ref, *rest, loads, sources, halves, first, first_half):
    kept, rest = rest[:sources], rest[sources:]
    *outs, queries, kv, scores, tangents, sem, query_sem = rest
    scale = HDIM**-0.5
    half, clip = pl.program_id(0), pl.program_id(1)
    start = (half == 0) & (clip == 0)
    split = 2 * HDIM
    blocks = [(h, c) for h in range(halves) for c in range(2)]

    def fetch(step, at):
        return pltpu.make_async_copy(
            q_ref.at[
                pl.ds((first + at[1]) * SENDERS, SENDERS),
                pl.ds((first_half + at[0]) * HALF, HALF),
            ],
            queries.at[step],
            query_sem.at[step],
        )

    def copies(part):
        lanes = pl.ds(part * split, split)
        return [
            pltpu.make_async_copy(
                kept[which].at[pl.ds(source * SENDERS, count * SENDERS), :, lanes],
                kv.at[pl.ds(target * SENDERS, count * SENDERS), :, lanes],
                sem.at[part, n],
            )
            for n, (which, source, target, count) in enumerate(loads)
        ]

    @pl.when(start)
    def _():
        fetches = [fetch(step, at) for step, at in enumerate(blocks)]
        for copy in copies(0) + fetches:
            copy.start()
        for copy in copies(0) + fetches:
            copy.wait()
        for copy in copies(1):
            copy.start()

    both = queries[2 * half + clip].reshape(BLOCK, 2 * HDIM)
    query = both[:, HDIM:]
    picks = [slots_ref[clip, n] * SENDERS for n in range(3)]
    tiles = [(n, k) for n in range(3) for k in range(0, CLIP, TILE)]

    def window(n, k, lanes):
        rows = pl.ds(picks[n] + k // 128, TILE // 128)
        return kv[rows, :, lanes].reshape(TILE, -1)

    top = None
    for n, k in tiles:
        part = lax.dot_general(query, window(n, k, slice(0, HDIM)), NT, preferred_element_type=f32)
        at = n * CLIP + k
        scores[:, at : at + TILE] = part
        for lane in range(0, TILE, HDIM):
            piece = part[:, lane : lane + HDIM]
            top = piece if top is None else jnp.maximum(top, piece)
    top = jnp.broadcast_to(jnp.max(top, axis=1, keepdims=True), (BLOCK, HDIM))
    total = jnp.zeros((BLOCK, HDIM), f32)
    mean = jnp.zeros((BLOCK, HDIM), f32)
    for n, k in tiles:
        tangent = lax.dot_general(
            both, window(n, k, slice(0, 2 * HDIM)), NT, preferred_element_type=f32
        )
        for lane in range(0, TILE, HDIM):
            at = n * CLIP + k + lane
            part = jnp.exp2((scores[:, at : at + HDIM] - top) * (scale * LOG2E))
            moved = part * tangent[:, lane : lane + HDIM]
            total += part
            mean += moved
            scores[:, at : at + HDIM] = part
            tangents[:, at : at + HDIM] = moved
    inverse = 1.0 / jnp.sum(total, axis=1, keepdims=True)
    mean = jnp.broadcast_to(jnp.sum(mean, axis=1, keepdims=True) * inverse, (BLOCK, HDIM))

    @pl.when(start)
    def _():
        for copy in copies(1):
            copy.wait()

    out = jnp.zeros((BLOCK, 2 * HDIM), f32)
    tan = jnp.zeros((BLOCK, HDIM), f32)
    for n, k in tiles:
        weights, weights_tan = [], []
        for lane in range(0, TILE, HDIM):
            at = n * CLIP + k + lane
            part = scores[:, at : at + HDIM]
            weights.append(part.astype(bf16))
            weights_tan.append((tangents[:, at : at + HDIM] - part * mean).astype(bf16))
        out += jnp.dot(
            jnp.concatenate(weights, axis=1),
            window(n, k, slice(2 * HDIM, 4 * HDIM)),
            preferred_element_type=f32,
        )
        tan += jnp.dot(
            jnp.concatenate(weights_tan, axis=1),
            window(n, k, slice(2 * HDIM, 3 * HDIM)),
            preferred_element_type=f32,
        )
    result = (out[:, :HDIM] * inverse).astype(bf16).reshape(SENDERS, HALF, HDIM)
    result_tan = ((tan * scale + out[:, HDIM:]) * inverse).astype(bf16)
    result_tan = result_tan.reshape(SENDERS, HALF, HDIM)

    pair_ref, sent_ref = outs
    pair_ref[0] = result
    sent_ref[:, :, :HDIM] = result
    sent_ref[:, :, HDIM:] = result_tan


def attend(slots, queries, kept, loads, late, first_half, halves, filled=None):
    first = 2 if late else 0
    in_specs = [pl.BlockSpec(memory_space=pl.ANY)] * (1 + len(kept) + (filled is not None))
    out_shape = (
        jax.ShapeDtypeStruct((halves, 16, HALF, HDIM), bf16),
        jax.ShapeDtypeStruct((32, 2 * HALF, 2 * HDIM), bf16),
    )
    out_specs = (
        pl.BlockSpec((1, SENDERS, HALF, HDIM), lambda h, c, s: (h, c, 0, 0)),
        pl.BlockSpec(
            (SENDERS, HALF, 2 * HDIM), lambda h, c, s: (first + c, first_half + h, 0)
        ),
    )
    operands = (slots, queries, *kept) + (() if filled is None else (filled,))
    return pl.pallas_call(
        functools.partial(
            attend_kernel,
            loads=loads,
            sources=len(kept) + (filled is not None),
            halves=halves,
            first=first,
            first_half=first_half,
        ),
        out_shape=out_shape,
        grid_spec=pltpu.PrefetchScalarGridSpec(
            num_scalar_prefetch=1,
            grid=(halves, 2),
            in_specs=in_specs,
            out_specs=out_specs,
            scratch_shapes=[
                pltpu.VMEM((2 * halves, SENDERS, HALF, 2 * HDIM), bf16),
                pltpu.VMEM((4 * SENDERS, 128, 4 * HDIM), bf16),
                pltpu.VMEM((BLOCK, 3 * CLIP), f32),
                pltpu.VMEM((BLOCK, 3 * CLIP), f32),
                pltpu.SemaphoreType.DMA((2, len(loads))),
                pltpu.SemaphoreType.DMA((2 * halves,)),
            ],
        ),
        input_output_aliases={} if filled is None else {len(operands) - 1: 1},
        compiler_params=pltpu.CompilerParams(
            dimension_semantics=("arbitrary", "arbitrary"), vmem_limit_bytes=28 << 20
        ),
        cost_estimate=pl.CostEstimate(
            flops=2 * 2 * halves * BLOCK * 3 * CLIP * HDIM * 8,
            transcendentals=2 * halves * BLOCK * 3 * CLIP,
            bytes_accessed=8 << 20,
        ),
    )(*operands)


def turn_kernel(ref, out_ref):
    out_ref[...] = ref[...].T


def turned(cotangent):
    rows, columns = cotangent.shape
    return pl.pallas_call(
        turn_kernel,
        out_shape=jax.ShapeDtypeStruct((columns, rows), bf16),
        grid=(8,),
        in_specs=[pl.BlockSpec((rows, columns // 8), lambda j: (0, j))],
        out_specs=pl.BlockSpec((columns // 8, rows), lambda j: (j, 0)),
        compiler_params=pltpu.CompilerParams(vmem_limit_bytes=32 << 20),
        cost_estimate=pl.CostEstimate(flops=0, transcendentals=0, bytes_accessed=24 << 20),
    )(cotangent)


def grad_kernel(place_ref, early_a, early_b, got_a, got_b, late, got_late, cot_ref, *rest):
    outs, (pair, rows, parts, sem, arrived, left) = rest[:8], rest[8:]
    plane, side = place_ref[0], place_ref[1]
    height = 2 * parts.shape[2]
    reads = [
        pltpu.make_async_copy(
            cot_ref.at[pl.ds(pl.multiple_of((plane + dx) % 4 * height, height), height)],
            rows.at[step],
            arrived.at[step],
        )
        for step, dx in enumerate(HOPS)
    ]
    reads[0].start()
    reads[1].start()

    def load(left_halves, right_halves):
        copies = []
        for column, halves in enumerate((left_halves, right_halves)):
            for half, ref in enumerate(halves):
                copies.append(
                    pltpu.make_async_copy(
                        ref,
                        pair.at[:, pl.ds(half * HALF, HALF), pl.ds(column * HDIM, HDIM)],
                        sem.at[2 * column + half],
                    )
                )
        for copy in copies:
            copy.start()
        for copy in copies:
            copy.wait()

    halves = lambda ref: (ref.at[0], ref.at[1])
    own = (early_a.at[0], early_b.at[0])
    far = (got_a.at[0], got_b.at[0])
    pl.when(side == 0)(lambda: load(own, far))
    pl.when(side == 1)(lambda: load(halves(got_late), halves(late)))
    writes = []
    for step, copy in enumerate(reads):
        copy.wait()
        if step + 2 < len(reads):
            reads[step + 2].start()
        for row in range(0, height, 128):
            part = jnp.dot(
                rows[step, row : row + 128],
                pair[...].reshape(2 * CLIP, 2 * HDIM),
                preferred_element_type=f32,
            )
            at = row % (height // 2)
            parts[step, 2 * row // height, at : at + 128] = part.astype(bf16)
        for dz in range(2):
            n = 2 * step + dz
            writes.append(
                pltpu.make_async_copy(parts.at[step, side ^ dz], outs[n], left.at[n])
            )
            writes[-1].start()
    for copy in writes:
        copy.wait()


def grad_terms(place, attended, cotangent):
    columns, rows = cotangent.shape
    width = columns // 8
    anywhere = pl.BlockSpec(memory_space=pl.ANY)
    return pl.pallas_call(
        grad_kernel,
        out_shape=[jax.ShapeDtypeStruct((width, 2 * HDIM), bf16)] * 8,
        grid_spec=pltpu.PrefetchScalarGridSpec(
            num_scalar_prefetch=1,
            grid=(),
            in_specs=[anywhere] * 7,
            out_specs=[anywhere] * 8,
            scratch_shapes=[
                pltpu.VMEM((16, 2 * HALF, 2 * HDIM), bf16),
                pltpu.VMEM((4, 2 * width, rows), bf16),
                pltpu.VMEM((4, 2, width, 2 * HDIM), bf16),
                pltpu.SemaphoreType.DMA((4,)),
                pltpu.SemaphoreType.DMA((4,)),
                pltpu.SemaphoreType.DMA((8,)),
            ],
        ),
        compiler_params=pltpu.CompilerParams(vmem_limit_bytes=56 << 20),
        cost_estimate=pl.CostEstimate(
            flops=2 * rows * columns * 2 * HDIM, transcendentals=0, bytes_accessed=15 << 20
        ),
    )(place, *attended, cotangent)


def on_device(
    queries, key_rows, value_rows, query_tangent, key_tangent, value_tangent, partners, cotangent
):
    own = to_heads(packed(key_rows, key_tangent, value_rows, value_tangent))
    halo = lax.ppermute(own[16:], "x", [(i, (i + 1) % 4) for i in range(4)])
    query, columns = lax.optimization_barrier((packed(query_tangent, queries), turned(cotangent)))
    query = to_heads(query)

    plane = lax.axis_index("x") * 4
    mine = lax.dynamic_slice_in_dim(partners, plane, 4, 0)
    near = (mine - plane + 2) % 16
    slots = jnp.concatenate([jnp.arange(2, 6, dtype=jnp.int32)[:, None], near], axis=1)
    late, sent = attend(slots[2:] - 2, query, (own,), ((0, 0, 0, 4),), True, 0, 2)
    window = ((1, 0, 0, 2), (0, 0, 2, 2))
    early1, sent = attend(slots[:2], query, (own, halo), window, False, 0, 1, sent)
    early2, sent = attend(slots[:2], query, (own, halo), window, False, 1, 1, sent)

    got_late = lax.ppermute(late, "zl", [(0, 1)])
    got1 = lax.ppermute(early1, "zl", [(1, 0)])
    last, *_ = lax.optimization_barrier((early2, got_late, got1))
    got2 = lax.ppermute(last, "zl", [(1, 0)])
    sent, _ = lax.optimization_barrier((sent, got2))
    back = lax.all_to_all(sent, PLANE, 0, 0, tiled=True)
    place = jnp.stack([lax.axis_index("x"), lax.axis_index("zl")]).astype(jnp.int32)
    terms = grad_terms(
        place, (early1, early2, got1, got2, late, got_late), columns
    )
    arrived = []
    for n, term in enumerate(terms):
        dx, dz = HOPS[n // 2], n % 2
        ring = [(2 * x + z, 2 * ((x + dx) % 4) + (z ^ dz)) for x in range(4) for z in range(2)]
        arrived.append(term if (dx, dz) == (0, 0) else lax.ppermute(term, CLIPS, ring))
    weight_grad = sum(term.astype(f32) for term in arrived)
    return *unpack(back), weight_grad


def solution(mesh):
    fine = Mesh(np.asarray(mesh.devices).reshape(4, 2, 2, 4, 2), EVERY)
    rows = P(EVERY, None)
    return jax.shard_map(
        on_device,
        mesh=fine,
        in_specs=(rows, rows, rows, rows, rows, rows, P(), P(CLIPS, None)),
        out_specs=(rows, rows, P(CLIPS, GROUP)),
        check_vma=False,
    )
```

```python
import functools

import jax
import jax.numpy as jnp
import numpy as np
from jax import lax
from jax.experimental import pallas as pl
from jax.experimental.pallas import tpu as pltpu
from jax.sharding import Mesh
from jax.sharding import PartitionSpec as P

HDIM = 128
CLIP = 1024
HEADS = 32
HALF = 64
SENDERS = 8
BLOCK = SENDERS * HALF
TILE = 256
HOPS = (2, 1, 3, 0)
LOG2E = 1.4426950408889634
PLANE = ("zl", "zh", "y", "c")
GROUP = ("zh", "y", "c")
CLIPS = ("x", "zl")
EVERY = ("x", "zl", "zh", "y", "c")
NT = (((1,), (1,)), ((), ()))
bf16, f32 = jnp.bfloat16, jnp.float32


def pack_kernel(*refs):
    count = len(refs) - 5
    ins, (out, rows, cut, arrived, left) = refs[:count], refs[count:]
    steps = arrived.shape[0]
    heads = HEADS // steps
    width = heads * HDIM
    reads = [
        [
            pltpu.make_async_copy(
                ref.at[:, pl.ds(step * width, width)],
                rows.at[n, :, pl.ds(step * width, width)],
                arrived.at[step, n],
            )
            for n, ref in enumerate(ins)
        ]
        for step in range(steps)
    ]
    for copies in reads:
        for copy in copies:
            copy.start()
    writes = []
    for step, copies in enumerate(reads):
        for n, copy in enumerate(copies):
            copy.wait()
            for head in range(step * heads, (step + 1) * heads):
                cut[head % 2, head // 2, :, n * HDIM : (n + 1) * HDIM] = rows[
                    n, :, head * HDIM : (head + 1) * HDIM
                ]
        part = pl.ds(step * heads // 2, heads // 2)
        writes.append(pltpu.make_async_copy(cut.at[:, part], out.at[:, part], left.at[step]))
        writes[-1].start()
    for copy in writes:
        copy.wait()


def packed(*arrays):
    count = len(arrays)
    rows, width = arrays[0].shape[0], count * HDIM
    steps = 4
    anywhere = pl.BlockSpec(memory_space=pl.ANY)
    return pl.pallas_call(
        pack_kernel,
        out_shape=jax.ShapeDtypeStruct((2, 16, rows, width), bf16),
        in_specs=[anywhere] * count,
        out_specs=anywhere,
        scratch_shapes=[
            pltpu.VMEM((count, rows, HEADS * HDIM), bf16),
            pltpu.VMEM((2, 16, rows, width), bf16),
            pltpu.SemaphoreType.DMA((steps, count)),
            pltpu.SemaphoreType.DMA((steps,)),
        ],
        compiler_params=pltpu.CompilerParams(vmem_limit_bytes=60 << 20),
        cost_estimate=pl.CostEstimate(
            flops=0, transcendentals=0, bytes_accessed=4 * rows * HEADS * width
        ),
    )(*arrays).reshape(32, rows, width)


def to_heads(sent):
    return lax.all_to_all(sent, PLANE, 0, 0, tiled=True)


def unpack_kernel(even_ref, odd_ref, out_ref, tan_ref):
    for head in range(8):
        lanes = slice(head * HDIM, (head + 1) * HDIM)
        ref = odd_ref if head % 2 else even_ref
        out_ref[:, lanes] = ref[head // 2, :, :HDIM]
        tan_ref[:, lanes] = ref[head // 2, :, HDIM:]


def unpack(back):
    rows = back.shape[1]
    shape = jax.ShapeDtypeStruct((rows, HEADS * HDIM), bf16)
    spec = pl.BlockSpec((rows, 8 * HDIM), lambda j: (0, j))
    return pl.pallas_call(
        unpack_kernel,
        out_shape=(shape, shape),
        grid=(4,),
        in_specs=[
            pl.BlockSpec((4, rows, 2 * HDIM), lambda j: (j, 0, 0)),
            pl.BlockSpec((4, rows, 2 * HDIM), lambda j: (4 + j, 0, 0)),
        ],
        out_specs=(spec, spec),
        compiler_params=pltpu.CompilerParams(vmem_limit_bytes=8 << 20),
        cost_estimate=pl.CostEstimate(flops=0, transcendentals=0, bytes_accessed=4 << 20),
    )(back, back)


def attend_kernel(slots_ref, q_ref, *rest, loads, sources, halves, first, first_half):
    kept, rest = rest[:sources], rest[sources:]
    *outs, queries, kv, scores, tangents, sem, query_sem = rest
    scale = HDIM**-0.5
    half, clip = pl.program_id(0), pl.program_id(1)
    start = (half == 0) & (clip == 0)
    split = 2 * HDIM
    blocks = [(h, c) for h in range(halves) for c in range(2)]

    def fetch(step, at):
        return pltpu.make_async_copy(
            q_ref.at[
                pl.ds((first + at[1]) * SENDERS, SENDERS),
                pl.ds((first_half + at[0]) * HALF, HALF),
            ],
            queries.at[step],
            query_sem.at[step],
        )

    def copies(part):
        lanes = pl.ds(part * split, split)
        return [
            pltpu.make_async_copy(
                kept[which].at[pl.ds(source * SENDERS, count * SENDERS), :, lanes],
                kv.at[pl.ds(target * SENDERS, count * SENDERS), :, lanes],
                sem.at[part, n],
            )
            for n, (which, source, target, count) in enumerate(loads)
        ]

    @pl.when(start)
    def _():
        fetches = [fetch(step, at) for step, at in enumerate(blocks)]
        for copy in copies(0) + fetches:
            copy.start()
        for copy in copies(0) + fetches:
            copy.wait()
        for copy in copies(1):
            copy.start()

    both = queries[2 * half + clip].reshape(BLOCK, 2 * HDIM)
    query = both[:, HDIM:]
    picks = [slots_ref[clip, n] * SENDERS for n in range(3)]
    tiles = [(n, k) for n in range(3) for k in range(0, CLIP, TILE)]

    def window(n, k, lanes):
        rows = pl.ds(picks[n] + k // 128, TILE // 128)
        return kv[rows, :, lanes].reshape(TILE, -1)

    top = None
    for n, k in tiles:
        part = lax.dot_general(query, window(n, k, slice(0, HDIM)), NT, preferred_element_type=f32)
        at = n * CLIP + k
        scores[:, at : at + TILE] = part
        for lane in range(0, TILE, HDIM):
            piece = part[:, lane : lane + HDIM]
            top = piece if top is None else jnp.maximum(top, piece)
    top = jnp.broadcast_to(jnp.max(top, axis=1, keepdims=True), (BLOCK, HDIM))
    total = jnp.zeros((BLOCK, HDIM), f32)
    mean = jnp.zeros((BLOCK, HDIM), f32)
    for n, k in tiles:
        tangent = lax.dot_general(
            both, window(n, k, slice(0, 2 * HDIM)), NT, preferred_element_type=f32
        )
        for lane in range(0, TILE, HDIM):
            at = n * CLIP + k + lane
            part = jnp.exp2((scores[:, at : at + HDIM] - top) * (scale * LOG2E))
            moved = part * tangent[:, lane : lane + HDIM]
            total += part
            mean += moved
            scores[:, at : at + HDIM] = part
            tangents[:, at : at + HDIM] = moved
    inverse = 1.0 / jnp.sum(total, axis=1, keepdims=True)
    mean = jnp.broadcast_to(jnp.sum(mean, axis=1, keepdims=True) * inverse, (BLOCK, HDIM))

    @pl.when(start)
    def _():
        for copy in copies(1):
            copy.wait()

    out = jnp.zeros((BLOCK, 2 * HDIM), f32)
    tan = jnp.zeros((BLOCK, HDIM), f32)
    for n, k in tiles:
        weights, weights_tan = [], []
        for lane in range(0, TILE, HDIM):
            at = n * CLIP + k + lane
            part = scores[:, at : at + HDIM]
            weights.append(part.astype(bf16))
            weights_tan.append((tangents[:, at : at + HDIM] - part * mean).astype(bf16))
        out += jnp.dot(
            jnp.concatenate(weights, axis=1),
            window(n, k, slice(2 * HDIM, 4 * HDIM)),
            preferred_element_type=f32,
        )
        tan += jnp.dot(
            jnp.concatenate(weights_tan, axis=1),
            window(n, k, slice(2 * HDIM, 3 * HDIM)),
            preferred_element_type=f32,
        )
    result = (out[:, :HDIM] * inverse).astype(bf16).reshape(SENDERS, HALF, HDIM)
    result_tan = ((tan * scale + out[:, HDIM:]) * inverse).astype(bf16)
    result_tan = result_tan.reshape(SENDERS, HALF, HDIM)

    pair_ref, sent_ref = outs
    pair_ref[0] = result
    sent_ref[:, :, :HDIM] = result
    sent_ref[:, :, HDIM:] = result_tan


def attend(slots, queries, kept, loads, late, first_half, halves, filled=None):
    first = 2 if late else 0
    in_specs = [pl.BlockSpec(memory_space=pl.ANY)] * (1 + len(kept) + (filled is not None))
    out_shape = (
        jax.ShapeDtypeStruct((halves, 16, HALF, HDIM), bf16),
        jax.ShapeDtypeStruct((32, 2 * HALF, 2 * HDIM), bf16),
    )
    out_specs = (
        pl.BlockSpec((1, SENDERS, HALF, HDIM), lambda h, c, s: (h, c, 0, 0)),
        pl.BlockSpec(
            (SENDERS, HALF, 2 * HDIM), lambda h, c, s: (first + c, first_half + h, 0)
        ),
    )
    operands = (slots, queries, *kept) + (() if filled is None else (filled,))
    return pl.pallas_call(
        functools.partial(
            attend_kernel,
            loads=loads,
            sources=len(kept) + (filled is not None),
            halves=halves,
            first=first,
            first_half=first_half,
        ),
        out_shape=out_shape,
        grid_spec=pltpu.PrefetchScalarGridSpec(
            num_scalar_prefetch=1,
            grid=(halves, 2),
            in_specs=in_specs,
            out_specs=out_specs,
            scratch_shapes=[
                pltpu.VMEM((2 * halves, SENDERS, HALF, 2 * HDIM), bf16),
                pltpu.VMEM((4 * SENDERS, 128, 4 * HDIM), bf16),
                pltpu.VMEM((BLOCK, 3 * CLIP), f32),
                pltpu.VMEM((BLOCK, 3 * CLIP), f32),
                pltpu.SemaphoreType.DMA((2, len(loads))),
                pltpu.SemaphoreType.DMA((2 * halves,)),
            ],
        ),
        input_output_aliases={} if filled is None else {len(operands) - 1: 1},
        compiler_params=pltpu.CompilerParams(
            dimension_semantics=("arbitrary", "arbitrary"), vmem_limit_bytes=28 << 20
        ),
        cost_estimate=pl.CostEstimate(
            flops=2 * 2 * halves * BLOCK * 3 * CLIP * HDIM * 8,
            transcendentals=2 * halves * BLOCK * 3 * CLIP,
            bytes_accessed=8 << 20,
        ),
    )(*operands)


def turn_kernel(ref, out_ref):
    out_ref[...] = ref[...].T


def turned(cotangent):
    rows, columns = cotangent.shape
    return pl.pallas_call(
        turn_kernel,
        out_shape=jax.ShapeDtypeStruct((columns, rows), bf16),
        grid=(8,),
        in_specs=[pl.BlockSpec((rows, columns // 8), lambda j: (0, j))],
        out_specs=pl.BlockSpec((columns // 8, rows), lambda j: (j, 0)),
        compiler_params=pltpu.CompilerParams(vmem_limit_bytes=32 << 20),
        cost_estimate=pl.CostEstimate(flops=0, transcendentals=0, bytes_accessed=24 << 20),
    )(cotangent)


def grad_kernel(place_ref, early_a, early_b, got_a, got_b, late, got_late, cot_ref, *rest):
    outs, (pair, rows, parts, sem, arrived, left) = rest[:8], rest[8:]
    plane, side = place_ref[0], place_ref[1]
    height = 2 * parts.shape[2]
    reads = [
        pltpu.make_async_copy(
            cot_ref.at[pl.ds(pl.multiple_of((plane + dx) % 4 * height, height), height)],
            rows.at[step],
            arrived.at[step],
        )
        for step, dx in enumerate(HOPS)
    ]
    reads[0].start()
    reads[1].start()

    def load(left_halves, right_halves):
        copies = []
        for column, halves in enumerate((left_halves, right_halves)):
            for half, ref in enumerate(halves):
                copies.append(
                    pltpu.make_async_copy(
                        ref,
                        pair.at[:, pl.ds(half * HALF, HALF), pl.ds(column * HDIM, HDIM)],
                        sem.at[2 * column + half],
                    )
                )
        for copy in copies:
            copy.start()
        for copy in copies:
            copy.wait()

    halves = lambda ref: (ref.at[0], ref.at[1])
    own = (early_a.at[0], early_b.at[0])
    far = (got_a.at[0], got_b.at[0])
    pl.when(side == 0)(lambda: load(own, far))
    pl.when(side == 1)(lambda: load(halves(got_late), halves(late)))
    writes = []
    for step, copy in enumerate(reads):
        copy.wait()
        if step + 2 < len(reads):
            reads[step + 2].start()
        for row in range(0, height, 128):
            part = jnp.dot(
                rows[step, row : row + 128],
                pair[...].reshape(2 * CLIP, 2 * HDIM),
                preferred_element_type=f32,
            )
            at = row % (height // 2)
            parts[step, 2 * row // height, at : at + 128] = part.astype(bf16)
        for dz in range(2):
            n = 2 * step + dz
            writes.append(
                pltpu.make_async_copy(parts.at[step, side ^ dz], outs[n], left.at[n])
            )
            writes[-1].start()
    for copy in writes:
        copy.wait()


def grad_terms(place, attended, cotangent):
    columns, rows = cotangent.shape
    width = columns // 8
    anywhere = pl.BlockSpec(memory_space=pl.ANY)
    return pl.pallas_call(
        grad_kernel,
        out_shape=[jax.ShapeDtypeStruct((width, 2 * HDIM), bf16)] * 8,
        grid_spec=pltpu.PrefetchScalarGridSpec(
            num_scalar_prefetch=1,
            grid=(),
            in_specs=[anywhere] * 7,
            out_specs=[anywhere] * 8,
            scratch_shapes=[
                pltpu.VMEM((16, 2 * HALF, 2 * HDIM), bf16),
                pltpu.VMEM((4, 2 * width, rows), bf16),
                pltpu.VMEM((4, 2, width, 2 * HDIM), bf16),
                pltpu.SemaphoreType.DMA((4,)),
                pltpu.SemaphoreType.DMA((4,)),
                pltpu.SemaphoreType.DMA((8,)),
            ],
        ),
        compiler_params=pltpu.CompilerParams(vmem_limit_bytes=56 << 20),
        cost_estimate=pl.CostEstimate(
            flops=2 * rows * columns * 2 * HDIM, transcendentals=0, bytes_accessed=15 << 20
        ),
    )(place, *attended, cotangent)


def on_device(
    queries, key_rows, value_rows, query_tangent, key_tangent, value_tangent, partners, cotangent
):
    own = to_heads(packed(key_rows, key_tangent, value_rows, value_tangent))
    halo = lax.ppermute(own[16:], "x", [(i, (i + 1) % 4) for i in range(4)])
    place = jnp.stack([lax.axis_index("x"), lax.axis_index("zl")]).astype(jnp.int32)
    query, columns, place = lax.optimization_barrier(
        (packed(query_tangent, queries), turned(cotangent), place)
    )
    query = to_heads(query)

    plane = lax.axis_index("x") * 4
    mine = lax.dynamic_slice_in_dim(partners, plane, 4, 0)
    near = (mine - plane + 2) % 16
    slots = jnp.concatenate([jnp.arange(2, 6, dtype=jnp.int32)[:, None], near], axis=1)
    late, sent = attend(slots[2:] - 2, query, (own,), ((0, 0, 0, 4),), True, 0, 2)
    window = ((1, 0, 0, 2), (0, 0, 2, 2))
    early1, sent = attend(slots[:2], query, (own, halo), window, False, 0, 1, sent)
    early2, sent = attend(slots[:2], query, (own, halo), window, False, 1, 1, sent)

    got_late = lax.ppermute(late, "zl", [(0, 1)])
    got1 = lax.ppermute(early1, "zl", [(1, 0)])
    last, *_ = lax.optimization_barrier((early2, got_late, got1))
    got2 = lax.ppermute(last, "zl", [(1, 0)])
    sent, _ = lax.optimization_barrier((sent, got2))
    back = lax.all_to_all(sent, PLANE, 0, 0, tiled=True)
    terms = grad_terms(
        place, (early1, early2, got1, got2, late, got_late), columns
    )
    arrived = []
    for n, term in enumerate(terms):
        dx, dz = HOPS[n // 2], n % 2
        ring = [(2 * x + z, 2 * ((x + dx) % 4) + (z ^ dz)) for x in range(4) for z in range(2)]
        arrived.append(term if (dx, dz) == (0, 0) else lax.ppermute(term, CLIPS, ring))
    rows, arrived = lax.optimization_barrier((unpack(back), arrived))
    weight_grad = sum(term.astype(f32) for term in arrived)
    return *rows, weight_grad


def solution(mesh):
    fine = Mesh(np.asarray(mesh.devices).reshape(4, 2, 2, 4, 2), EVERY)
    rows = P(EVERY, None)
    return jax.shard_map(
        on_device,
        mesh=fine,
        in_specs=(rows, rows, rows, rows, rows, rows, P(), P(CLIPS, None)),
        out_specs=(rows, rows, P(CLIPS, GROUP)),
        check_vma=False,
    )
```

```python
import functools

import jax
import jax.numpy as jnp
import numpy as np
from jax import lax
from jax.experimental import pallas as pl
from jax.experimental.pallas import tpu as pltpu
from jax.sharding import Mesh
from jax.sharding import PartitionSpec as P

HDIM = 128
CLIP = 1024
HEADS = 32
HALF = 64
SENDERS = 8
BLOCK = SENDERS * HALF
TILE = 256
HOPS = (2, 1, 3, 0)
LOG2E = 1.4426950408889634
PLANE = ("zl", "zh", "y", "c")
GROUP = ("zh", "y", "c")
CLIPS = ("x", "zl")
EVERY = ("x", "zl", "zh", "y", "c")
NT = (((1,), (1,)), ((), ()))
bf16, f32 = jnp.bfloat16, jnp.float32


def pack_kernel(*refs):
    count = len(refs) - 5
    ins, (out, rows, cut, arrived, left) = refs[:count], refs[count:]
    steps = arrived.shape[0]
    heads = HEADS // steps
    width = heads * HDIM
    reads = [
        [
            pltpu.make_async_copy(
                ref.at[:, pl.ds(step * width, width)],
                rows.at[n, :, pl.ds(step * width, width)],
                arrived.at[step, n],
            )
            for n, ref in enumerate(ins)
        ]
        for step in range(steps)
    ]
    for copies in reads:
        for copy in copies:
            copy.start()
    writes = []
    for step, copies in enumerate(reads):
        for n, copy in enumerate(copies):
            copy.wait()
            for head in range(step * heads, (step + 1) * heads):
                cut[head % 2, head // 2, :, n * HDIM : (n + 1) * HDIM] = rows[
                    n, :, head * HDIM : (head + 1) * HDIM
                ]
        part = pl.ds(step * heads // 2, heads // 2)
        writes.append(pltpu.make_async_copy(cut.at[:, part], out.at[:, part], left.at[step]))
        writes[-1].start()
    for copy in writes:
        copy.wait()


def packed(*arrays):
    count = len(arrays)
    rows, width = arrays[0].shape[0], count * HDIM
    steps = 4
    anywhere = pl.BlockSpec(memory_space=pl.ANY)
    return pl.pallas_call(
        pack_kernel,
        out_shape=jax.ShapeDtypeStruct((2, 16, rows, width), bf16),
        in_specs=[anywhere] * count,
        out_specs=anywhere,
        scratch_shapes=[
            pltpu.VMEM((count, rows, HEADS * HDIM), bf16),
            pltpu.VMEM((2, 16, rows, width), bf16),
            pltpu.SemaphoreType.DMA((steps, count)),
            pltpu.SemaphoreType.DMA((steps,)),
        ],
        compiler_params=pltpu.CompilerParams(vmem_limit_bytes=60 << 20),
        cost_estimate=pl.CostEstimate(
            flops=0, transcendentals=0, bytes_accessed=4 * rows * HEADS * width
        ),
    )(*arrays).reshape(32, rows, width)


def to_heads(sent):
    return lax.all_to_all(sent, PLANE, 0, 0, tiled=True)


def unpack_kernel(even_ref, odd_ref, out_ref, tan_ref):
    for head in range(8):
        lanes = slice(head * HDIM, (head + 1) * HDIM)
        ref = odd_ref if head % 2 else even_ref
        out_ref[:, lanes] = ref[head // 2, :, :HDIM]
        tan_ref[:, lanes] = ref[head // 2, :, HDIM:]


def unpack(back):
    rows = back.shape[1]
    shape = jax.ShapeDtypeStruct((rows, HEADS * HDIM), bf16)
    spec = pl.BlockSpec((rows, 8 * HDIM), lambda j: (0, j))
    return pl.pallas_call(
        unpack_kernel,
        out_shape=(shape, shape),
        grid=(4,),
        in_specs=[
            pl.BlockSpec((4, rows, 2 * HDIM), lambda j: (j, 0, 0)),
            pl.BlockSpec((4, rows, 2 * HDIM), lambda j: (4 + j, 0, 0)),
        ],
        out_specs=(spec, spec),
        compiler_params=pltpu.CompilerParams(vmem_limit_bytes=8 << 20),
        cost_estimate=pl.CostEstimate(flops=0, transcendentals=0, bytes_accessed=4 << 20),
    )(back, back)


def attend_kernel(slots_ref, q_ref, *rest, loads, sources, halves, first, first_half):
    kept, rest = rest[:sources], rest[sources:]
    *outs, queries, kv, scores, tangents, sem, query_sem = rest
    scale = HDIM**-0.5
    half, clip = pl.program_id(0), pl.program_id(1)
    start = (half == 0) & (clip == 0)
    split = 2 * HDIM
    blocks = [(h, c) for h in range(halves) for c in range(2)]

    def fetch(step, at):
        return pltpu.make_async_copy(
            q_ref.at[
                pl.ds((first + at[1]) * SENDERS, SENDERS),
                pl.ds((first_half + at[0]) * HALF, HALF),
            ],
            queries.at[step],
            query_sem.at[step],
        )

    def copies(part):
        lanes = pl.ds(part * split, split)
        return [
            pltpu.make_async_copy(
                kept[which].at[pl.ds(source * SENDERS, count * SENDERS), :, lanes],
                kv.at[pl.ds(target * SENDERS, count * SENDERS), :, lanes],
                sem.at[part, n],
            )
            for n, (which, source, target, count) in enumerate(loads)
        ]

    @pl.when(start)
    def _():
        fetches = [fetch(step, at) for step, at in enumerate(blocks)]
        for copy in copies(0) + fetches:
            copy.start()
        for copy in copies(0) + fetches:
            copy.wait()
        for copy in copies(1):
            copy.start()

    both = queries[2 * half + clip].reshape(BLOCK, 2 * HDIM)
    query = both[:, HDIM:]
    picks = [slots_ref[clip, n] * SENDERS for n in range(3)]
    tiles = [(n, k) for n in range(3) for k in range(0, CLIP, TILE)]

    def window(n, k, lanes):
        rows = pl.ds(picks[n] + k // 128, TILE // 128)
        return kv[rows, :, lanes].reshape(TILE, -1)

    top = None
    for n, k in tiles:
        part = lax.dot_general(query, window(n, k, slice(0, HDIM)), NT, preferred_element_type=f32)
        at = n * CLIP + k
        scores[:, at : at + TILE] = part
        for lane in range(0, TILE, HDIM):
            piece = part[:, lane : lane + HDIM]
            top = piece if top is None else jnp.maximum(top, piece)
    top = jnp.broadcast_to(jnp.max(top, axis=1, keepdims=True), (BLOCK, HDIM))
    total = jnp.zeros((BLOCK, HDIM), f32)
    mean = jnp.zeros((BLOCK, HDIM), f32)
    for n, k in tiles:
        tangent = lax.dot_general(
            both, window(n, k, slice(0, 2 * HDIM)), NT, preferred_element_type=f32
        )
        for lane in range(0, TILE, HDIM):
            at = n * CLIP + k + lane
            part = jnp.exp2((scores[:, at : at + HDIM] - top) * (scale * LOG2E))
            moved = part * tangent[:, lane : lane + HDIM]
            total += part
            mean += moved
            scores[:, at : at + HDIM] = part
            tangents[:, at : at + HDIM] = moved
    inverse = 1.0 / jnp.sum(total, axis=1, keepdims=True)
    mean = jnp.broadcast_to(jnp.sum(mean, axis=1, keepdims=True) * inverse, (BLOCK, HDIM))

    @pl.when(start)
    def _():
        for copy in copies(1):
            copy.wait()

    out = jnp.zeros((BLOCK, 2 * HDIM), f32)
    tan = jnp.zeros((BLOCK, HDIM), f32)
    for n, k in tiles:
        weights, weights_tan = [], []
        for lane in range(0, TILE, HDIM):
            at = n * CLIP + k + lane
            part = scores[:, at : at + HDIM]
            weights.append(part.astype(bf16))
            weights_tan.append((tangents[:, at : at + HDIM] - part * mean).astype(bf16))
        out += jnp.dot(
            jnp.concatenate(weights, axis=1),
            window(n, k, slice(2 * HDIM, 4 * HDIM)),
            preferred_element_type=f32,
        )
        tan += jnp.dot(
            jnp.concatenate(weights_tan, axis=1),
            window(n, k, slice(2 * HDIM, 3 * HDIM)),
            preferred_element_type=f32,
        )
    result = (out[:, :HDIM] * inverse).astype(bf16).reshape(SENDERS, HALF, HDIM)
    result_tan = ((tan * scale + out[:, HDIM:]) * inverse).astype(bf16)
    result_tan = result_tan.reshape(SENDERS, HALF, HDIM)

    pair_ref, sent_ref = outs
    pair_ref[0] = result
    sent_ref[:, :, :HDIM] = result
    sent_ref[:, :, HDIM:] = result_tan


def attend(slots, queries, kept, loads, late, first_half, halves, filled=None):
    first = 2 if late else 0
    in_specs = [pl.BlockSpec(memory_space=pl.ANY)] * (1 + len(kept) + (filled is not None))
    out_shape = (
        jax.ShapeDtypeStruct((halves, 16, HALF, HDIM), bf16),
        jax.ShapeDtypeStruct((32, 2 * HALF, 2 * HDIM), bf16),
    )
    out_specs = (
        pl.BlockSpec((1, SENDERS, HALF, HDIM), lambda h, c, s: (h, c, 0, 0)),
        pl.BlockSpec(
            (SENDERS, HALF, 2 * HDIM), lambda h, c, s: (first + c, first_half + h, 0)
        ),
    )
    operands = (slots, queries, *kept) + (() if filled is None else (filled,))
    return pl.pallas_call(
        functools.partial(
            attend_kernel,
            loads=loads,
            sources=len(kept) + (filled is not None),
            halves=halves,
            first=first,
            first_half=first_half,
        ),
        out_shape=out_shape,
        grid_spec=pltpu.PrefetchScalarGridSpec(
            num_scalar_prefetch=1,
            grid=(halves, 2),
            in_specs=in_specs,
            out_specs=out_specs,
            scratch_shapes=[
                pltpu.VMEM((2 * halves, SENDERS, HALF, 2 * HDIM), bf16),
                pltpu.VMEM((4 * SENDERS, 128, 4 * HDIM), bf16),
                pltpu.VMEM((BLOCK, 3 * CLIP), f32),
                pltpu.VMEM((BLOCK, 3 * CLIP), f32),
                pltpu.SemaphoreType.DMA((2, len(loads))),
                pltpu.SemaphoreType.DMA((2 * halves,)),
            ],
        ),
        input_output_aliases={} if filled is None else {len(operands) - 1: 1},
        compiler_params=pltpu.CompilerParams(
            dimension_semantics=("arbitrary", "arbitrary"), vmem_limit_bytes=28 << 20
        ),
        cost_estimate=pl.CostEstimate(
            flops=2 * 2 * halves * BLOCK * 3 * CLIP * HDIM * 8,
            transcendentals=2 * halves * BLOCK * 3 * CLIP,
            bytes_accessed=8 << 20,
        ),
    )(*operands)


def turn_kernel(ref, out_ref):
    out_ref[...] = ref[...].T


def turned(cotangent):
    rows, columns = cotangent.shape
    return pl.pallas_call(
        turn_kernel,
        out_shape=jax.ShapeDtypeStruct((columns, rows), bf16),
        grid=(8,),
        in_specs=[pl.BlockSpec((rows, columns // 8), lambda j: (0, j))],
        out_specs=pl.BlockSpec((columns // 8, rows), lambda j: (j, 0)),
        compiler_params=pltpu.CompilerParams(vmem_limit_bytes=32 << 20),
        cost_estimate=pl.CostEstimate(flops=0, transcendentals=0, bytes_accessed=24 << 20),
    )(cotangent)


def grad_kernel(place_ref, early_a, early_b, got_a, got_b, late, got_late, cot_ref, *rest):
    outs, (pair, rows, parts, sem, arrived, left) = rest[:8], rest[8:]
    plane, side = place_ref[0], place_ref[1]
    height = 2 * parts.shape[2]
    reads = [
        pltpu.make_async_copy(
            cot_ref.at[pl.ds(pl.multiple_of((plane + dx) % 4 * height, height), height)],
            rows.at[step],
            arrived.at[step],
        )
        for step, dx in enumerate(HOPS)
    ]
    reads[0].start()
    reads[1].start()

    def load(left_halves, right_halves):
        copies = []
        for column, halves in enumerate((left_halves, right_halves)):
            for half, ref in enumerate(halves):
                copies.append(
                    pltpu.make_async_copy(
                        ref,
                        pair.at[:, pl.ds(half * HALF, HALF), pl.ds(column * HDIM, HDIM)],
                        sem.at[2 * column + half],
                    )
                )
        for copy in copies:
            copy.start()
        for copy in copies:
            copy.wait()

    halves = lambda ref: (ref.at[0], ref.at[1])
    own = (early_a.at[0], early_b.at[0])
    far = (got_a.at[0], got_b.at[0])
    pl.when(side == 0)(lambda: load(own, far))
    pl.when(side == 1)(lambda: load(halves(got_late), halves(late)))
    writes = []
    for step, copy in enumerate(reads):
        copy.wait()
        if step + 2 < len(reads):
            reads[step + 2].start()
        for row in range(0, height, 128):
            part = jnp.dot(
                rows[step, row : row + 128],
                pair[...].reshape(2 * CLIP, 2 * HDIM),
                preferred_element_type=f32,
            )
            at = row % (height // 2)
            parts[step, 2 * row // height, at : at + 128] = part.astype(bf16)
        for dz in range(2):
            n = 2 * step + dz
            writes.append(
                pltpu.make_async_copy(parts.at[step, side ^ dz], outs[n], left.at[n])
            )
            writes[-1].start()
    for copy in writes:
        copy.wait()


def grad_terms(place, attended, cotangent):
    columns, rows = cotangent.shape
    width = columns // 8
    anywhere = pl.BlockSpec(memory_space=pl.ANY)
    return pl.pallas_call(
        grad_kernel,
        out_shape=[jax.ShapeDtypeStruct((width, 2 * HDIM), bf16)] * 8,
        grid_spec=pltpu.PrefetchScalarGridSpec(
            num_scalar_prefetch=1,
            grid=(),
            in_specs=[anywhere] * 7,
            out_specs=[anywhere] * 8,
            scratch_shapes=[
                pltpu.VMEM((16, 2 * HALF, 2 * HDIM), bf16),
                pltpu.VMEM((4, 2 * width, rows), bf16),
                pltpu.VMEM((4, 2, width, 2 * HDIM), bf16),
                pltpu.SemaphoreType.DMA((4,)),
                pltpu.SemaphoreType.DMA((4,)),
                pltpu.SemaphoreType.DMA((8,)),
            ],
        ),
        compiler_params=pltpu.CompilerParams(vmem_limit_bytes=56 << 20),
        cost_estimate=pl.CostEstimate(
            flops=2 * rows * columns * 2 * HDIM, transcendentals=0, bytes_accessed=15 << 20
        ),
    )(place, *attended, cotangent)


def on_device(
    queries, key_rows, value_rows, query_tangent, key_tangent, value_tangent, partners, cotangent
):
    own = to_heads(packed(key_rows, key_tangent, value_rows, value_tangent))
    halo = lax.ppermute(own[16:], "x", [(i, (i + 1) % 4) for i in range(4)])
    place = jnp.stack([lax.axis_index("x"), lax.axis_index("zl")]).astype(jnp.int32)
    query, columns, place = lax.optimization_barrier(
        (packed(query_tangent, queries), turned(cotangent), place)
    )
    query = to_heads(query)

    plane = lax.axis_index("x") * 4
    mine = lax.dynamic_slice_in_dim(partners, plane, 4, 0)
    near = (mine - plane + 2) % 16
    slots = jnp.concatenate([jnp.arange(2, 6, dtype=jnp.int32)[:, None], near], axis=1)
    late, sent = attend(slots[2:] - 2, query, (own,), ((0, 0, 0, 4),), True, 0, 2)
    window = ((1, 0, 0, 2), (0, 0, 2, 2))
    early1, sent = attend(slots[:2], query, (own, halo), window, False, 0, 1, sent)
    early2, sent = attend(slots[:2], query, (own, halo), window, False, 1, 1, sent)

    got_late = lax.ppermute(late, "zl", [(0, 1)])
    got1 = lax.ppermute(early1, "zl", [(1, 0)])
    last, *_ = lax.optimization_barrier((early2, got_late, got1))
    got2 = lax.ppermute(last, "zl", [(1, 0)])
    sent, _ = lax.optimization_barrier((sent, got2))
    back = lax.all_to_all(sent, PLANE, 0, 0, tiled=True)
    terms = grad_terms(
        place, (early1, early2, got1, got2, late, got_late), columns
    )
    arrived = []
    for dz in (1, 0):
        for step, dx in enumerate(HOPS):
            term = terms[2 * step + dz]
            ring = [(2 * x + z, 2 * ((x + dx) % 4) + (z ^ dz)) for x in range(4) for z in range(2)]
            arrived.append(term if (dx, dz) == (0, 0) else lax.ppermute(term, CLIPS, ring))
    weight_grad = sum(term.astype(f32) for term in arrived)
    return *unpack(back), weight_grad


def solution(mesh):
    fine = Mesh(np.asarray(mesh.devices).reshape(4, 2, 2, 4, 2), EVERY)
    rows = P(EVERY, None)
    return jax.shard_map(
        on_device,
        mesh=fine,
        in_specs=(rows, rows, rows, rows, rows, rows, P(), P(CLIPS, None)),
        out_specs=(rows, rows, P(CLIPS, GROUP)),
        check_vma=False,
    )
```

```python
import functools

import jax
import jax.numpy as jnp
import numpy as np
from jax import lax
from jax.experimental import pallas as pl
from jax.experimental.pallas import tpu as pltpu
from jax.sharding import Mesh
from jax.sharding import PartitionSpec as P

HDIM = 128
CLIP = 1024
HEADS = 32
HALF = 64
SENDERS = 8
BLOCK = SENDERS * HALF
TILE = 256
HOPS = (2, 1, 3, 0)
LOG2E = 1.4426950408889634
PLANE = ("zl", "zh", "y", "c")
GROUP = ("zh", "y", "c")
CLIPS = ("x", "zl")
EVERY = ("x", "zl", "zh", "y", "c")
NT = (((1,), (1,)), ((), ()))
bf16, f32 = jnp.bfloat16, jnp.float32


def pack_kernel(*refs):
    count = len(refs) - 5
    ins, (out, rows, cut, arrived, left) = refs[:count], refs[count:]
    steps = arrived.shape[0]
    heads = HEADS // steps
    width = heads * HDIM
    reads = [
        [
            pltpu.make_async_copy(
                ref.at[:, pl.ds(step * width, width)],
                rows.at[n, :, pl.ds(step * width, width)],
                arrived.at[step, n],
            )
            for n, ref in enumerate(ins)
        ]
        for step in range(steps)
    ]
    for copies in reads:
        for copy in copies:
            copy.start()
    writes = []
    for step, copies in enumerate(reads):
        for n, copy in enumerate(copies):
            copy.wait()
            for head in range(step * heads, (step + 1) * heads):
                cut[head % 2, head // 2, :, n * HDIM : (n + 1) * HDIM] = rows[
                    n, :, head * HDIM : (head + 1) * HDIM
                ]
        part = pl.ds(step * heads // 2, heads // 2)
        writes.append(pltpu.make_async_copy(cut.at[:, part], out.at[:, part], left.at[step]))
        writes[-1].start()
    for copy in writes:
        copy.wait()


def packed(*arrays):
    count = len(arrays)
    rows, width = arrays[0].shape[0], count * HDIM
    steps = 4
    anywhere = pl.BlockSpec(memory_space=pl.ANY)
    return pl.pallas_call(
        pack_kernel,
        out_shape=jax.ShapeDtypeStruct((2, 16, rows, width), bf16),
        in_specs=[anywhere] * count,
        out_specs=anywhere,
        scratch_shapes=[
            pltpu.VMEM((count, rows, HEADS * HDIM), bf16),
            pltpu.VMEM((2, 16, rows, width), bf16),
            pltpu.SemaphoreType.DMA((steps, count)),
            pltpu.SemaphoreType.DMA((steps,)),
        ],
        compiler_params=pltpu.CompilerParams(vmem_limit_bytes=60 << 20),
        cost_estimate=pl.CostEstimate(
            flops=0, transcendentals=0, bytes_accessed=4 * rows * HEADS * width
        ),
    )(*arrays).reshape(32, rows, width)


def to_heads(sent):
    return lax.all_to_all(sent, PLANE, 0, 0, tiled=True)


def unpack_kernel(even_ref, odd_ref, out_ref, tan_ref):
    for head in range(8):
        lanes = slice(head * HDIM, (head + 1) * HDIM)
        ref = odd_ref if head % 2 else even_ref
        out_ref[:, lanes] = ref[head // 2, :, :HDIM]
        tan_ref[:, lanes] = ref[head // 2, :, HDIM:]


def unpack(back):
    rows = back.shape[1]
    shape = jax.ShapeDtypeStruct((rows, HEADS * HDIM), bf16)
    spec = pl.BlockSpec((rows, 8 * HDIM), lambda j: (0, j))
    return pl.pallas_call(
        unpack_kernel,
        out_shape=(shape, shape),
        grid=(4,),
        in_specs=[
            pl.BlockSpec((4, rows, 2 * HDIM), lambda j: (j, 0, 0)),
            pl.BlockSpec((4, rows, 2 * HDIM), lambda j: (4 + j, 0, 0)),
        ],
        out_specs=(spec, spec),
        compiler_params=pltpu.CompilerParams(vmem_limit_bytes=8 << 20),
        cost_estimate=pl.CostEstimate(flops=0, transcendentals=0, bytes_accessed=4 << 20),
    )(back, back)


def attend_kernel(slots_ref, q_ref, *rest, loads, sources, halves, first, first_half):
    kept, rest = rest[:sources], rest[sources:]
    *outs, queries, kv, scores, tangents, sem, query_sem = rest
    scale = HDIM**-0.5
    half, clip = pl.program_id(0), pl.program_id(1)
    start = (half == 0) & (clip == 0)
    split = 2 * HDIM
    blocks = [(h, c) for h in range(halves) for c in range(2)]

    def fetch(step, at):
        return pltpu.make_async_copy(
            q_ref.at[
                pl.ds((first + at[1]) * SENDERS, SENDERS),
                pl.ds((first_half + at[0]) * HALF, HALF),
            ],
            queries.at[step],
            query_sem.at[step],
        )

    def copies(part):
        lanes = pl.ds(part * split, split)
        return [
            pltpu.make_async_copy(
                kept[which].at[pl.ds(source * SENDERS, count * SENDERS), :, lanes],
                kv.at[pl.ds(target * SENDERS, count * SENDERS), :, lanes],
                sem.at[part, n],
            )
            for n, (which, source, target, count) in enumerate(loads)
        ]

    @pl.when(start)
    def _():
        fetches = [fetch(step, at) for step, at in enumerate(blocks)]
        for copy in copies(0) + fetches:
            copy.start()
        for copy in copies(0) + fetches:
            copy.wait()
        for copy in copies(1):
            copy.start()

    both = queries[2 * half + clip].reshape(BLOCK, 2 * HDIM)
    query = both[:, HDIM:]
    picks = [slots_ref[clip, n] * SENDERS for n in range(3)]
    tiles = [(n, k) for n in range(3) for k in range(0, CLIP, TILE)]

    def window(n, k, lanes):
        rows = pl.ds(picks[n] + k // 128, TILE // 128)
        return kv[rows, :, lanes].reshape(TILE, -1)

    top = None
    for n, k in tiles:
        part = lax.dot_general(query, window(n, k, slice(0, HDIM)), NT, preferred_element_type=f32)
        at = n * CLIP + k
        scores[:, at : at + TILE] = part
        for lane in range(0, TILE, HDIM):
            piece = part[:, lane : lane + HDIM]
            top = piece if top is None else jnp.maximum(top, piece)
    top = jnp.broadcast_to(jnp.max(top, axis=1, keepdims=True), (BLOCK, HDIM))
    total = jnp.zeros((BLOCK, HDIM), f32)
    mean = jnp.zeros((BLOCK, HDIM), f32)
    for n, k in tiles:
        tangent = lax.dot_general(
            both, window(n, k, slice(0, 2 * HDIM)), NT, preferred_element_type=f32
        )
        for lane in range(0, TILE, HDIM):
            at = n * CLIP + k + lane
            part = jnp.exp2((scores[:, at : at + HDIM] - top) * (scale * LOG2E))
            moved = part * tangent[:, lane : lane + HDIM]
            total += part
            mean += moved
            scores[:, at : at + HDIM] = part
            tangents[:, at : at + HDIM] = moved
    inverse = 1.0 / jnp.sum(total, axis=1, keepdims=True)
    mean = jnp.broadcast_to(jnp.sum(mean, axis=1, keepdims=True) * inverse, (BLOCK, HDIM))

    @pl.when(start)
    def _():
        for copy in copies(1):
            copy.wait()

    out = jnp.zeros((BLOCK, 2 * HDIM), f32)
    tan = jnp.zeros((BLOCK, HDIM), f32)
    for n, k in tiles:
        weights, weights_tan = [], []
        for lane in range(0, TILE, HDIM):
            at = n * CLIP + k + lane
            part = scores[:, at : at + HDIM]
            weights.append(part.astype(bf16))
            weights_tan.append((tangents[:, at : at + HDIM] - part * mean).astype(bf16))
        out += jnp.dot(
            jnp.concatenate(weights, axis=1),
            window(n, k, slice(2 * HDIM, 4 * HDIM)),
            preferred_element_type=f32,
        )
        tan += jnp.dot(
            jnp.concatenate(weights_tan, axis=1),
            window(n, k, slice(2 * HDIM, 3 * HDIM)),
            preferred_element_type=f32,
        )
    result = (out[:, :HDIM] * inverse).astype(bf16).reshape(SENDERS, HALF, HDIM)
    result_tan = ((tan * scale + out[:, HDIM:]) * inverse).astype(bf16)
    result_tan = result_tan.reshape(SENDERS, HALF, HDIM)

    pair_ref, sent_ref = outs
    pair_ref[0] = result
    sent_ref[:, :, :HDIM] = result
    sent_ref[:, :, HDIM:] = result_tan


def attend(slots, queries, kept, loads, late, first_half, halves, filled=None):
    first = 2 if late else 0
    in_specs = [pl.BlockSpec(memory_space=pl.ANY)] * (1 + len(kept) + (filled is not None))
    out_shape = (
        jax.ShapeDtypeStruct((halves, 16, HALF, HDIM), bf16),
        jax.ShapeDtypeStruct((32, 2 * HALF, 2 * HDIM), bf16),
    )
    out_specs = (
        pl.BlockSpec((1, SENDERS, HALF, HDIM), lambda h, c, s: (h, c, 0, 0)),
        pl.BlockSpec(
            (SENDERS, HALF, 2 * HDIM), lambda h, c, s: (first + c, first_half + h, 0)
        ),
    )
    operands = (slots, queries, *kept) + (() if filled is None else (filled,))
    return pl.pallas_call(
        functools.partial(
            attend_kernel,
            loads=loads,
            sources=len(kept) + (filled is not None),
            halves=halves,
            first=first,
            first_half=first_half,
        ),
        out_shape=out_shape,
        grid_spec=pltpu.PrefetchScalarGridSpec(
            num_scalar_prefetch=1,
            grid=(halves, 2),
            in_specs=in_specs,
            out_specs=out_specs,
            scratch_shapes=[
                pltpu.VMEM((2 * halves, SENDERS, HALF, 2 * HDIM), bf16),
                pltpu.VMEM((4 * SENDERS, 128, 4 * HDIM), bf16),
                pltpu.VMEM((BLOCK, 3 * CLIP), f32),
                pltpu.VMEM((BLOCK, 3 * CLIP), f32),
                pltpu.SemaphoreType.DMA((2, len(loads))),
                pltpu.SemaphoreType.DMA((2 * halves,)),
            ],
        ),
        input_output_aliases={} if filled is None else {len(operands) - 1: 1},
        compiler_params=pltpu.CompilerParams(
            dimension_semantics=("arbitrary", "arbitrary"), vmem_limit_bytes=28 << 20
        ),
        cost_estimate=pl.CostEstimate(
            flops=2 * 2 * halves * BLOCK * 3 * CLIP * HDIM * 8,
            transcendentals=2 * halves * BLOCK * 3 * CLIP,
            bytes_accessed=8 << 20,
        ),
    )(*operands)


def turn_kernel(ref, out_ref):
    out_ref[...] = ref[...].T


def turned(cotangent):
    rows, columns = cotangent.shape
    return pl.pallas_call(
        turn_kernel,
        out_shape=jax.ShapeDtypeStruct((columns, rows), bf16),
        grid=(8,),
        in_specs=[pl.BlockSpec((rows, columns // 8), lambda j: (0, j))],
        out_specs=pl.BlockSpec((columns // 8, rows), lambda j: (j, 0)),
        compiler_params=pltpu.CompilerParams(vmem_limit_bytes=32 << 20),
        cost_estimate=pl.CostEstimate(flops=0, transcendentals=0, bytes_accessed=24 << 20),
    )(cotangent)


def grad_kernel(place_ref, early_a, early_b, got_a, got_b, late, got_late, cot_ref, *rest):
    outs, (pair, rows, parts, sem, arrived, left) = rest[:8], rest[8:]
    plane, side = place_ref[0], place_ref[1]
    height = 2 * parts.shape[2]
    reads = [
        pltpu.make_async_copy(
            cot_ref.at[pl.ds(pl.multiple_of((plane + dx) % 4 * height, height), height)],
            rows.at[step],
            arrived.at[step],
        )
        for step, dx in enumerate(HOPS)
    ]
    reads[0].start()
    reads[1].start()

    def load(left_halves, right_halves):
        copies = []
        for column, halves in enumerate((left_halves, right_halves)):
            for half, ref in enumerate(halves):
                copies.append(
                    pltpu.make_async_copy(
                        ref,
                        pair.at[:, pl.ds(half * HALF, HALF), pl.ds(column * HDIM, HDIM)],
                        sem.at[2 * column + half],
                    )
                )
        for copy in copies:
            copy.start()
        for copy in copies:
            copy.wait()

    halves = lambda ref: (ref.at[0], ref.at[1])
    own = (early_a.at[0], early_b.at[0])
    far = (got_a.at[0], got_b.at[0])
    pl.when(side == 0)(lambda: load(own, far))
    pl.when(side == 1)(lambda: load(halves(got_late), halves(late)))
    writes = []
    for step, copy in enumerate(reads):
        copy.wait()
        if step + 2 < len(reads):
            reads[step + 2].start()
        for row in range(0, height, 128):
            part = jnp.dot(
                rows[step, row : row + 128],
                pair[...].reshape(2 * CLIP, 2 * HDIM),
                preferred_element_type=f32,
            )
            at = row % (height // 2)
            parts[step, 2 * row // height, at : at + 128] = part.astype(bf16)
        for dz in range(2):
            n = 2 * step + dz
            writes.append(
                pltpu.make_async_copy(parts.at[step, side ^ dz], outs[n], left.at[n])
            )
            writes[-1].start()
    for copy in writes:
        copy.wait()


def grad_terms(place, attended, cotangent):
    columns, rows = cotangent.shape
    width = columns // 8
    anywhere = pl.BlockSpec(memory_space=pl.ANY)
    return pl.pallas_call(
        grad_kernel,
        out_shape=[jax.ShapeDtypeStruct((width, 2 * HDIM), bf16)] * 8,
        grid_spec=pltpu.PrefetchScalarGridSpec(
            num_scalar_prefetch=1,
            grid=(),
            in_specs=[anywhere] * 7,
            out_specs=[anywhere] * 8,
            scratch_shapes=[
                pltpu.VMEM((16, 2 * HALF, 2 * HDIM), bf16),
                pltpu.VMEM((4, 2 * width, rows), bf16),
                pltpu.VMEM((4, 2, width, 2 * HDIM), bf16),
                pltpu.SemaphoreType.DMA((4,)),
                pltpu.SemaphoreType.DMA((4,)),
                pltpu.SemaphoreType.DMA((8,)),
            ],
        ),
        compiler_params=pltpu.CompilerParams(vmem_limit_bytes=56 << 20),
        cost_estimate=pl.CostEstimate(
            flops=2 * rows * columns * 2 * HDIM, transcendentals=0, bytes_accessed=15 << 20
        ),
    )(place, *attended, cotangent)


def on_device(
    queries, key_rows, value_rows, query_tangent, key_tangent, value_tangent, partners, cotangent
):
    own = to_heads(packed(key_rows, key_tangent, value_rows, value_tangent))
    halo = lax.ppermute(own[16:], "x", [(i, (i + 1) % 4) for i in range(4)])
    place = jnp.stack([lax.axis_index("x"), lax.axis_index("zl")]).astype(jnp.int32)
    query, columns, place = lax.optimization_barrier(
        (packed(query_tangent, queries), turned(cotangent), place)
    )
    query = to_heads(query)

    plane = lax.axis_index("x") * 4
    mine = lax.dynamic_slice_in_dim(partners, plane, 4, 0)
    near = (mine - plane + 2) % 16
    slots = jnp.concatenate([jnp.arange(2, 6, dtype=jnp.int32)[:, None], near], axis=1)
    late, sent = attend(slots[2:] - 2, query, (own,), ((0, 0, 0, 4),), True, 0, 2)
    window = ((1, 0, 0, 2), (0, 0, 2, 2))
    early1, sent = attend(slots[:2], query, (own, halo), window, False, 0, 1, sent)
    early2, sent = attend(slots[:2], query, (own, halo), window, False, 1, 1, sent)

    got_late = lax.ppermute(late, "zl", [(0, 1)])
    got1 = lax.ppermute(early1, "zl", [(1, 0)])
    last, *_ = lax.optimization_barrier((early2, got_late, got1))
    got2 = lax.ppermute(last, "zl", [(1, 0)])
    sent, _ = lax.optimization_barrier((sent, got2))
    back = lax.all_to_all(sent, PLANE, 0, 0, tiled=True)
    terms = grad_terms(
        place, (early1, early2, got1, got2, late, got_late), columns
    )
    arrived = []
    for dx, dz in ((2, 0), (1, 0), (2, 1), (1, 1), (3, 1), (0, 1), (3, 0), (0, 0)):
        term = terms[2 * HOPS.index(dx) + dz]
        ring = [(2 * x + z, 2 * ((x + dx) % 4) + (z ^ dz)) for x in range(4) for z in range(2)]
        arrived.append(term if (dx, dz) == (0, 0) else lax.ppermute(term, CLIPS, ring))
    rows, arrived = lax.optimization_barrier((unpack(back), arrived))
    weight_grad = sum(term.astype(f32) for term in arrived)
    return *rows, weight_grad


def solution(mesh):
    fine = Mesh(np.asarray(mesh.devices).reshape(4, 2, 2, 4, 2), EVERY)
    rows = P(EVERY, None)
    return jax.shard_map(
        on_device,
        mesh=fine,
        in_specs=(rows, rows, rows, rows, rows, rows, P(), P(CLIPS, None)),
        out_specs=(rows, rows, P(CLIPS, GROUP)),
        check_vma=False,
    )
```

```python
import functools

import jax
import jax.numpy as jnp
import numpy as np
from jax import lax
from jax.experimental import pallas as pl
from jax.experimental.pallas import tpu as pltpu
from jax.sharding import Mesh
from jax.sharding import PartitionSpec as P

HDIM = 128
CLIP = 1024
HEADS = 32
HALF = 64
SENDERS = 8
BLOCK = SENDERS * HALF
TILE = 256
HOPS = (2, 1, 3, 0)
LOG2E = 1.4426950408889634
PLANE = ("zl", "zh", "y", "c")
GROUP = ("zh", "y", "c")
CLIPS = ("x", "zl")
EVERY = ("x", "zl", "zh", "y", "c")
NT = (((1,), (1,)), ((), ()))
bf16, f32 = jnp.bfloat16, jnp.float32


def pack_kernel(*refs):
    count = len(refs) - 5
    ins, (out, rows, cut, arrived, left) = refs[:count], refs[count:]
    steps = arrived.shape[0]
    heads = HEADS // steps
    width = heads * HDIM
    reads = [
        [
            pltpu.make_async_copy(
                ref.at[:, pl.ds(step * width, width)],
                rows.at[n, :, pl.ds(step * width, width)],
                arrived.at[step, n],
            )
            for n, ref in enumerate(ins)
        ]
        for step in range(steps)
    ]
    for copies in reads:
        for copy in copies:
            copy.start()
    writes = []
    for step, copies in enumerate(reads):
        for n, copy in enumerate(copies):
            copy.wait()
            for head in range(step * heads, (step + 1) * heads):
                cut[head % 2, head // 2, :, n * HDIM : (n + 1) * HDIM] = rows[
                    n, :, head * HDIM : (head + 1) * HDIM
                ]
        part = pl.ds(step * heads // 2, heads // 2)
        writes.append(pltpu.make_async_copy(cut.at[:, part], out.at[:, part], left.at[step]))
        writes[-1].start()
    for copy in writes:
        copy.wait()


def packed(*arrays):
    count = len(arrays)
    rows, width = arrays[0].shape[0], count * HDIM
    steps = 4
    anywhere = pl.BlockSpec(memory_space=pl.ANY)
    return pl.pallas_call(
        pack_kernel,
        out_shape=jax.ShapeDtypeStruct((2, 16, rows, width), bf16),
        in_specs=[anywhere] * count,
        out_specs=anywhere,
        scratch_shapes=[
            pltpu.VMEM((count, rows, HEADS * HDIM), bf16),
            pltpu.VMEM((2, 16, rows, width), bf16),
            pltpu.SemaphoreType.DMA((steps, count)),
            pltpu.SemaphoreType.DMA((steps,)),
        ],
        compiler_params=pltpu.CompilerParams(vmem_limit_bytes=60 << 20),
        cost_estimate=pl.CostEstimate(
            flops=0, transcendentals=0, bytes_accessed=4 * rows * HEADS * width
        ),
    )(*arrays).reshape(32, rows, width)


def to_heads(sent):
    return lax.all_to_all(sent, PLANE, 0, 0, tiled=True)


def unpack_kernel(even_ref, odd_ref, out_ref, tan_ref):
    for head in range(8):
        lanes = slice(head * HDIM, (head + 1) * HDIM)
        ref = odd_ref if head % 2 else even_ref
        out_ref[:, lanes] = ref[head // 2, :, :HDIM]
        tan_ref[:, lanes] = ref[head // 2, :, HDIM:]


def unpack(back):
    rows = back.shape[1]
    shape = jax.ShapeDtypeStruct((rows, HEADS * HDIM), bf16)
    spec = pl.BlockSpec((rows, 8 * HDIM), lambda j: (0, j))
    return pl.pallas_call(
        unpack_kernel,
        out_shape=(shape, shape),
        grid=(4,),
        in_specs=[
            pl.BlockSpec((4, rows, 2 * HDIM), lambda j: (j, 0, 0)),
            pl.BlockSpec((4, rows, 2 * HDIM), lambda j: (4 + j, 0, 0)),
        ],
        out_specs=(spec, spec),
        compiler_params=pltpu.CompilerParams(vmem_limit_bytes=8 << 20),
        cost_estimate=pl.CostEstimate(flops=0, transcendentals=0, bytes_accessed=4 << 20),
    )(back, back)


def attend_kernel(slots_ref, q_ref, *rest, loads, sources, halves, first, first_half):
    kept, rest = rest[:sources], rest[sources:]
    *outs, queries, kv, scores, tangents, sem, query_sem = rest
    scale = HDIM**-0.5
    half, clip = pl.program_id(0), pl.program_id(1)
    start = (half == 0) & (clip == 0)
    split = 2 * HDIM
    blocks = [(h, c) for h in range(halves) for c in range(2)]

    def fetch(step, at):
        return pltpu.make_async_copy(
            q_ref.at[
                pl.ds((first + at[1]) * SENDERS, SENDERS),
                pl.ds((first_half + at[0]) * HALF, HALF),
            ],
            queries.at[step],
            query_sem.at[step],
        )

    def copies(part):
        lanes = pl.ds(part * split, split)
        return [
            pltpu.make_async_copy(
                kept[which].at[pl.ds(source * SENDERS, count * SENDERS), :, lanes],
                kv.at[pl.ds(target * SENDERS, count * SENDERS), :, lanes],
                sem.at[part, n],
            )
            for n, (which, source, target, count) in enumerate(loads)
        ]

    @pl.when(start)
    def _():
        fetches = [fetch(step, at) for step, at in enumerate(blocks)]
        for copy in copies(0) + fetches:
            copy.start()
        for copy in copies(0) + fetches:
            copy.wait()
        for copy in copies(1):
            copy.start()

    both = queries[2 * half + clip].reshape(BLOCK, 2 * HDIM)
    query = both[:, HDIM:]
    picks = [slots_ref[clip, n] * SENDERS for n in range(3)]
    tiles = [(n, k) for n in range(3) for k in range(0, CLIP, TILE)]

    def window(n, k, lanes):
        rows = pl.ds(picks[n] + k // 128, TILE // 128)
        return kv[rows, :, lanes].reshape(TILE, -1)

    top = None
    for n, k in tiles:
        part = lax.dot_general(query, window(n, k, slice(0, HDIM)), NT, preferred_element_type=f32)
        at = n * CLIP + k
        scores[:, at : at + TILE] = part
        for lane in range(0, TILE, HDIM):
            piece = part[:, lane : lane + HDIM]
            top = piece if top is None else jnp.maximum(top, piece)
    top = jnp.broadcast_to(jnp.max(top, axis=1, keepdims=True), (BLOCK, HDIM))
    total = jnp.zeros((BLOCK, HDIM), f32)
    mean = jnp.zeros((BLOCK, HDIM), f32)
    for n, k in tiles:
        tangent = lax.dot_general(
            both, window(n, k, slice(0, 2 * HDIM)), NT, preferred_element_type=f32
        )
        for lane in range(0, TILE, HDIM):
            at = n * CLIP + k + lane
            part = jnp.exp2((scores[:, at : at + HDIM] - top) * (scale * LOG2E))
            moved = part * tangent[:, lane : lane + HDIM]
            total += part
            mean += moved
            scores[:, at : at + HDIM] = part
            tangents[:, at : at + HDIM] = moved
    inverse = 1.0 / jnp.sum(total, axis=1, keepdims=True)
    mean = jnp.broadcast_to(jnp.sum(mean, axis=1, keepdims=True) * inverse, (BLOCK, HDIM))

    @pl.when(start)
    def _():
        for copy in copies(1):
            copy.wait()

    out = jnp.zeros((BLOCK, 2 * HDIM), f32)
    tan = jnp.zeros((BLOCK, HDIM), f32)
    for n, k in tiles:
        weights, weights_tan = [], []
        for lane in range(0, TILE, HDIM):
            at = n * CLIP + k + lane
            part = scores[:, at : at + HDIM]
            weights.append(part.astype(bf16))
            weights_tan.append((tangents[:, at : at + HDIM] - part * mean).astype(bf16))
        out += jnp.dot(
            jnp.concatenate(weights, axis=1),
            window(n, k, slice(2 * HDIM, 4 * HDIM)),
            preferred_element_type=f32,
        )
        tan += jnp.dot(
            jnp.concatenate(weights_tan, axis=1),
            window(n, k, slice(2 * HDIM, 3 * HDIM)),
            preferred_element_type=f32,
        )
    result = (out[:, :HDIM] * inverse).astype(bf16).reshape(SENDERS, HALF, HDIM)
    result_tan = ((tan * scale + out[:, HDIM:]) * inverse).astype(bf16)
    result_tan = result_tan.reshape(SENDERS, HALF, HDIM)

    pair_ref, sent_ref = outs
    pair_ref[0] = result
    sent_ref[:, :, :HDIM] = result
    sent_ref[:, :, HDIM:] = result_tan


def attend(slots, queries, kept, loads, late, first_half, halves, filled=None):
    first = 2 if late else 0
    in_specs = [pl.BlockSpec(memory_space=pl.ANY)] * (1 + len(kept) + (filled is not None))
    out_shape = (
        jax.ShapeDtypeStruct((halves, 16, HALF, HDIM), bf16),
        jax.ShapeDtypeStruct((32, 2 * HALF, 2 * HDIM), bf16),
    )
    out_specs = (
        pl.BlockSpec((1, SENDERS, HALF, HDIM), lambda h, c, s: (h, c, 0, 0)),
        pl.BlockSpec(
            (SENDERS, HALF, 2 * HDIM), lambda h, c, s: (first + c, first_half + h, 0)
        ),
    )
    operands = (slots, queries, *kept) + (() if filled is None else (filled,))
    return pl.pallas_call(
        functools.partial(
            attend_kernel,
            loads=loads,
            sources=len(kept) + (filled is not None),
            halves=halves,
            first=first,
            first_half=first_half,
        ),
        out_shape=out_shape,
        grid_spec=pltpu.PrefetchScalarGridSpec(
            num_scalar_prefetch=1,
            grid=(halves, 2),
            in_specs=in_specs,
            out_specs=out_specs,
            scratch_shapes=[
                pltpu.VMEM((2 * halves, SENDERS, HALF, 2 * HDIM), bf16),
                pltpu.VMEM((4 * SENDERS, 128, 4 * HDIM), bf16),
                pltpu.VMEM((BLOCK, 3 * CLIP), f32),
                pltpu.VMEM((BLOCK, 3 * CLIP), f32),
                pltpu.SemaphoreType.DMA((2, len(loads))),
                pltpu.SemaphoreType.DMA((2 * halves,)),
            ],
        ),
        input_output_aliases={} if filled is None else {len(operands) - 1: 1},
        compiler_params=pltpu.CompilerParams(
            dimension_semantics=("arbitrary", "arbitrary"), vmem_limit_bytes=28 << 20
        ),
        cost_estimate=pl.CostEstimate(
            flops=2 * 2 * halves * BLOCK * 3 * CLIP * HDIM * 8,
            transcendentals=2 * halves * BLOCK * 3 * CLIP,
            bytes_accessed=8 << 20,
        ),
    )(*operands)


def turn_kernel(ref, out_ref):
    out_ref[...] = ref[...].T


def turned(cotangent):
    rows, columns = cotangent.shape
    return pl.pallas_call(
        turn_kernel,
        out_shape=jax.ShapeDtypeStruct((columns, rows), bf16),
        grid=(8,),
        in_specs=[pl.BlockSpec((rows, columns // 8), lambda j: (0, j))],
        out_specs=pl.BlockSpec((columns // 8, rows), lambda j: (j, 0)),
        compiler_params=pltpu.CompilerParams(vmem_limit_bytes=32 << 20),
        cost_estimate=pl.CostEstimate(flops=0, transcendentals=0, bytes_accessed=24 << 20),
    )(cotangent)


def grad_kernel(place_ref, early_a, early_b, got_a, got_b, late, got_late, cot_ref, *rest):
    outs, (pair, rows, parts, sem, arrived, left) = rest[:8], rest[8:]
    plane, side = place_ref[0], place_ref[1]
    height = 2 * parts.shape[2]
    reads = [
        pltpu.make_async_copy(
            cot_ref.at[pl.ds(pl.multiple_of((plane + dx) % 4 * height, height), height)],
            rows.at[step],
            arrived.at[step],
        )
        for step, dx in enumerate(HOPS)
    ]
    reads[0].start()
    reads[1].start()

    def load(left_halves, right_halves):
        copies = []
        for column, halves in enumerate((left_halves, right_halves)):
            for half, ref in enumerate(halves):
                copies.append(
                    pltpu.make_async_copy(
                        ref,
                        pair.at[:, pl.ds(half * HALF, HALF), pl.ds(column * HDIM, HDIM)],
                        sem.at[2 * column + half],
                    )
                )
        for copy in copies:
            copy.start()
        for copy in copies:
            copy.wait()

    halves = lambda ref: (ref.at[0], ref.at[1])
    own = (early_a.at[0], early_b.at[0])
    far = (got_a.at[0], got_b.at[0])
    pl.when(side == 0)(lambda: load(own, far))
    pl.when(side == 1)(lambda: load(halves(got_late), halves(late)))
    writes = []
    for step, copy in enumerate(reads):
        copy.wait()
        if step + 2 < len(reads):
            reads[step + 2].start()
        for row in range(0, height, 192):
            part = jnp.dot(
                rows[step, row : row + 192],
                pair[...].reshape(2 * CLIP, 2 * HDIM),
                preferred_element_type=f32,
            )
            at = row % (height // 2)
            parts[step, 2 * row // height, at : at + 192] = part.astype(bf16)
        for dz in range(2):
            n = 2 * step + dz
            writes.append(
                pltpu.make_async_copy(parts.at[step, side ^ dz], outs[n], left.at[n])
            )
            writes[-1].start()
    for copy in writes:
        copy.wait()


def grad_terms(place, attended, cotangent):
    columns, rows = cotangent.shape
    width = columns // 8
    anywhere = pl.BlockSpec(memory_space=pl.ANY)
    return pl.pallas_call(
        grad_kernel,
        out_shape=[jax.ShapeDtypeStruct((width, 2 * HDIM), bf16)] * 8,
        grid_spec=pltpu.PrefetchScalarGridSpec(
            num_scalar_prefetch=1,
            grid=(),
            in_specs=[anywhere] * 7,
            out_specs=[anywhere] * 8,
            scratch_shapes=[
                pltpu.VMEM((16, 2 * HALF, 2 * HDIM), bf16),
                pltpu.VMEM((4, 2 * width, rows), bf16),
                pltpu.VMEM((4, 2, width, 2 * HDIM), bf16),
                pltpu.SemaphoreType.DMA((4,)),
                pltpu.SemaphoreType.DMA((4,)),
                pltpu.SemaphoreType.DMA((8,)),
            ],
        ),
        compiler_params=pltpu.CompilerParams(vmem_limit_bytes=56 << 20),
        cost_estimate=pl.CostEstimate(
            flops=2 * rows * columns * 2 * HDIM, transcendentals=0, bytes_accessed=15 << 20
        ),
    )(place, *attended, cotangent)


def on_device(
    queries, key_rows, value_rows, query_tangent, key_tangent, value_tangent, partners, cotangent
):
    own = to_heads(packed(key_rows, key_tangent, value_rows, value_tangent))
    halo = lax.ppermute(own[16:], "x", [(i, (i + 1) % 4) for i in range(4)])
    place = jnp.stack([lax.axis_index("x"), lax.axis_index("zl")]).astype(jnp.int32)
    query, columns, place = lax.optimization_barrier(
        (packed(query_tangent, queries), turned(cotangent), place)
    )
    query = to_heads(query)

    plane = lax.axis_index("x") * 4
    mine = lax.dynamic_slice_in_dim(partners, plane, 4, 0)
    near = (mine - plane + 2) % 16
    slots = jnp.concatenate([jnp.arange(2, 6, dtype=jnp.int32)[:, None], near], axis=1)
    late, sent = attend(slots[2:] - 2, query, (own,), ((0, 0, 0, 4),), True, 0, 2)
    window = ((1, 0, 0, 2), (0, 0, 2, 2))
    early1, sent = attend(slots[:2], query, (own, halo), window, False, 0, 1, sent)
    early2, sent = attend(slots[:2], query, (own, halo), window, False, 1, 1, sent)

    got_late = lax.ppermute(late, "zl", [(0, 1)])
    got1 = lax.ppermute(early1, "zl", [(1, 0)])
    last, *_ = lax.optimization_barrier((early2, got_late, got1))
    got2 = lax.ppermute(last, "zl", [(1, 0)])
    sent, _ = lax.optimization_barrier((sent, got2))
    back = lax.all_to_all(sent, PLANE, 0, 0, tiled=True)
    terms = grad_terms(
        place, (early1, early2, got1, got2, late, got_late), columns
    )
    arrived = []
    for dx, dz in ((2, 0), (1, 0), (2, 1), (1, 1), (3, 1), (0, 1), (3, 0), (0, 0)):
        term = terms[2 * HOPS.index(dx) + dz]
        ring = [(2 * x + z, 2 * ((x + dx) % 4) + (z ^ dz)) for x in range(4) for z in range(2)]
        arrived.append(term if (dx, dz) == (0, 0) else lax.ppermute(term, CLIPS, ring))
    rows, arrived = lax.optimization_barrier((unpack(back), arrived))
    weight_grad = sum(term.astype(f32) for term in arrived)
    return *rows, weight_grad


def solution(mesh):
    fine = Mesh(np.asarray(mesh.devices).reshape(4, 2, 2, 4, 2), EVERY)
    rows = P(EVERY, None)
    return jax.shard_map(
        on_device,
        mesh=fine,
        in_specs=(rows, rows, rows, rows, rows, rows, P(), P(CLIPS, None)),
        out_specs=(rows, rows, P(CLIPS, GROUP)),
        check_vma=False,
    )
```
